512 devices in a mesh: seq: 64 (over z, x), tp: 8 (over y, core).
Axes of the slice: x: 4, y: 4, z: 16, core: 2. Of those that a mesh axis runs over, the one named last changes fastest.
Arguments:
- cache_keys: bfloat16 [131072, 2048], P('seq', 'tp'), may hold values from -13 to 13
- cache_values: bfloat16 [131072, 2048], P('seq', 'tp'), may hold values from -12 to 12
- keep_flags: int32 [131072], P('seq'), may hold values from 0 to 1, as said below
- drop_weight: int32 [131072], P('seq'), may hold values from 1 to 255
- req_blocks: int32 [48], replicated, may hold values from 1 to 128, 1024 in all
- queries: bfloat16 [48, 2048], P(None, 'tp'), may hold values from -48 to 48
- new_keys: bfloat16 [48, 2048], P(None, 'tp'), may hold values from -12 to 12
- new_values: bfloat16 [48, 2048], P(None, 'tp'), may hold values from -12 to 12
- out_weight: bfloat16 [2048, 2048], P('tp', 'seq'), may hold values from -0.125 to 0.125
Outputs:
- packed_keys: bfloat16 [66560, 2048], P('seq', 'tp')
- packed_values: bfloat16 [66560, 2048], P('seq', 'tp')
- packed_bias: bfloat16 [66560], P('seq')
- packed_request: int32 [66560], P('seq')
- layer_output: bfloat16 [48, 2048], P('tp', 'seq')
The draws below stay inside these ranges and needn't reach their ends.
Inputs may be any that keep to these rules, and one draw needn't show every extreme that they name: `keep_flags`: every aligned block of 128 rows keeps between 32 and 64 rows; in every draw all blocks of the rows of some one index of seq keep exactly 64. `req_blocks`: the entries sum to 1024; the largest is 128.
All inputs are finite; a program needn't handle non-finite values.
Results may differ from the reference program's by a relative error of at most 0.009.
Values may be sent and summed in bfloat16 or wider, within the bound.
A program may use at most 64 MiB of HBM per device.

```python
import math
import jax
import jax.numpy as jnp
import numpy as np
from jax import lax

D = 2048
HEADS = 8
HD = 256
BLOCK = 128
ROWS_DEV = 2048
REQS = 48
ROWS = 131072
TOTAL_BLOCKS = 1024
LONG_BLOCKS = 128
K_DEV = 1040
SLOTS = 66560
N_SEQ = 64


def shared_direction(key):
    signs = jax.random.normal(jax.random.fold_in(key, 7), (D,), jnp.float32)
    return jnp.where(signs >= 0.0, 2.0, -2.0).astype(jnp.float32)


def draw_cache_keys(key, part):
    drawn = jnp.clip(2.0 * jax.random.normal(jax.random.fold_in(key, 11), (ROWS, D), jnp.float32), -12.0, 12.0)
    direction = shared_direction(key)
    positions = jnp.arange(ROWS, dtype=jnp.int32)
    marked = positions % 97 == 0
    factor = 1.0 + 0.01 * (positions // 97 % 8).astype(jnp.float32)
    drawn = jnp.where(marked[:, None], direction[None, :] * factor[:, None], drawn)
    return drawn.astype(jnp.bfloat16)


def draw_queries(key, part):
    drawn = jnp.clip(jax.random.normal(jax.random.fold_in(key, 13), (REQS, D), jnp.float32), -6.0, 6.0)
    direction = shared_direction(key)
    chosen = jax.random.bernoulli(jax.random.fold_in(key, 17), 0.5, (REQS,))
    strength = jax.random.uniform(jax.random.fold_in(key, 19), (REQS,), jnp.float32, 25.0, 45.0)
    aligned = direction[None, :] * (strength / jnp.sqrt(jnp.float32(HD)))[:, None]
    drawn = jnp.where(chosen[:, None], aligned, drawn)
    return drawn.astype(jnp.bfloat16)


def draw_keep_flags(key, part):
    block_count = ROWS // BLOCK
    counts = jax.random.randint(jax.random.fold_in(key, 23), (block_count,), BLOCK // 4, BLOCK // 2 + 1)
    full_device = jax.random.randint(jax.random.fold_in(key, 29), (), 0, ROWS // ROWS_DEV)
    block_device = jnp.arange(block_count, dtype=jnp.int32) // (ROWS_DEV // BLOCK)
    counts = jnp.where(block_device == full_device, BLOCK // 2, counts)
    noise = jax.random.randint(jax.random.fold_in(key, 31), (block_count, BLOCK), 0, 2 ** 20)
    ranked = noise * BLOCK + jnp.arange(BLOCK, dtype=jnp.int32)[None, :]
    order = jnp.argsort(ranked, axis=1)
    position_rank = jnp.argsort(order, axis=1)
    return (position_rank < counts[:, None]).astype(jnp.int32).reshape(ROWS)


def set_ends(drawn, stream_key, low, top_value):
    spot = [jax.random.randint(jax.random.fold_in(stream_key, axis), (), 0, length) for axis, length in enumerate(drawn.shape)]
    widest = drawn.shape.index(max(drawn.shape))
    neighbour = spot[:widest] + [(spot[widest] + 1) % drawn.shape[widest]] + spot[widest + 1:]
    return drawn.at[tuple(spot)].set(low).at[tuple(neighbour)].set(top_value)


def block_scale(key, dims, cuts, smallest, largest):
    factor_of = 1.0
    for axis_at, blocks in cuts:
        draws = jax.random.uniform(jax.random.fold_in(jax.random.fold_in(key, 6), axis_at), (blocks,), jnp.float32, smallest / len(cuts), largest / len(cuts))
        factor_of = factor_of * jnp.repeat(jnp.exp(draws), dims[axis_at] // blocks).reshape((-1,) + (1,) * (len(dims) - 1 - axis_at))
    return factor_of


def profile(number_of, total, most, slope):
    weights = [(1 << 20) // math.isqrt(grade ** slope) + 1 for grade in range(2, number_of + 1)]
    spare, given = total - most - (number_of - 1), [1] * (number_of - 1)
    while spare > 0:
        movable = [i for i in range(number_of - 1) if given[i] < most]
        whole, left = sum([weights[i] for i in movable]), spare
        for i in movable:
            more = min(most - given[i], max(1, left * weights[i] // whole), spare)
            given[i] = given[i] + more
            spare = spare - more
    return np.array([most] + given)


def uneven(own_key, count, total, bound, lean):
    if count == 2:
        one = jax.random.randint(own_key, (), max(1, total - bound), min(bound, total - 1) + 1)
        return jnp.stack([one, total - one])
    lengths = jnp.asarray(profile(count, total, bound, lean), jnp.int32)
    twos = (count - 1) // 2
    source_of, receiver = lengths[1:1 + 2 * twos:2], lengths[2:2 + 2 * twos:2]
    margin = jnp.minimum(source_of - 1, bound - receiver)
    shifted = jax.random.randint(jax.random.fold_in(own_key, 1), (twos,), 0, 1 << 20) % (margin + 1)
    lengths = lengths.at[1:1 + 2 * twos:2].set(source_of - shifted).at[2:2 + 2 * twos:2].set(receiver + shifted)
    return lengths[jax.random.permutation(jax.random.fold_in(own_key, 2), count)]


def gaussian(own_key, dims, spread, bound, cuts=(), kind=jnp.bfloat16):
    factor_of = block_scale(own_key, dims, cuts, -0.22, 0.18) if cuts else 1.0
    array = jax.random.normal(own_key, dims, jnp.float32) * spread * factor_of
    return jnp.minimum(jnp.maximum(array, -bound), bound).astype(kind)


def setup_inputs(seed: int = 0) -> dict:
    arg_keys = jax.random.split(jax.random.key(seed), 10)
    return {
        "cache_keys": draw_cache_keys(jax.random.fold_in(arg_keys[9], 71), 0),
        "cache_values": gaussian(arg_keys[1], (ROWS, D), 2.0, 12.0, ((0, 64), (1, 8))),
        "keep_flags": draw_keep_flags(jax.random.fold_in(arg_keys[9], 71), 0),
        "drop_weight": set_ends(jax.random.randint(arg_keys[3], (ROWS,), 1, 256), jax.random.fold_in(arg_keys[3], 1), 1, 255).astype(jnp.int32),
        "req_blocks": uneven(arg_keys[4], REQS, TOTAL_BLOCKS, LONG_BLOCKS, 2).astype(jnp.int32),
        "queries": draw_queries(jax.random.fold_in(arg_keys[9], 71), 0),
        "new_keys": gaussian(arg_keys[6], (REQS, D), 2.0, 12.0, ((1, 8),)),
        "new_values": gaussian(arg_keys[7], (REQS, D), 2.0, 12.0, ((1, 8),)),
        "out_weight": gaussian(arg_keys[8], (D, D), D ** -0.5, 0.125, ((0, 8), (1, 64))),
    }


def fold_cache(cache, keep_flags, drop_weight):
    blocks_dev = ROWS_DEV // BLOCK
    weights = (drop_weight * (1 - keep_flags)).astype(jnp.float32).reshape(N_SEQ, blocks_dev, BLOCK)
    pieces = cache.reshape(N_SEQ, blocks_dev, BLOCK, cache.shape[1])

    def one_group(operands):
        group_weights, group_rows = operands
        summed = jnp.einsum('bi,bid->bd', group_weights, group_rows.astype(jnp.float32), precision=lax.Precision.HIGHEST)
        return summed / lax.optimization_barrier(jnp.sum(group_weights, axis=1))[:, None]
    folded = lax.map(one_group, (weights, pieces))
    return folded.reshape(-1, cache.shape[1]).astype(jnp.bfloat16)

def reference(cache_keys, cache_values, keep_flags, drop_weight, req_blocks, queries, new_keys, new_values, out_weight):
    block_count = ROWS // BLOCK
    keep_blocks = keep_flags.reshape(block_count, BLOCK)
    kept_count = lax.optimization_barrier(jnp.sum(keep_blocks, axis=1)).astype(jnp.int32)
    within = (jnp.cumsum(keep_blocks, axis=1) - keep_blocks).astype(jnp.int32)
    block_size = kept_count + 1
    block_base = (jnp.cumsum(block_size) - block_size).astype(jnp.int32)
    request_ends = jnp.cumsum(req_blocks).astype(jnp.int32)
    block_index = jnp.arange(block_count, dtype=jnp.int32)
    block_request = lax.optimization_barrier(jnp.sum((block_index[:, None] >= request_ends[None, :]).astype(jnp.int32), axis=1)).astype(jnp.int32)
    slot_count = SLOTS
    row_rank = (block_base[:, None] + within).reshape(-1)
    fold_rank = block_base + kept_count

    def place(global_rank):
        return (global_rank % N_SEQ * K_DEV + global_rank // N_SEQ).astype(jnp.int32)
    row_slot = jnp.where(keep_flags == 1, place(row_rank), slot_count).astype(jnp.int32)
    fold_slot = place(fold_rank)
    folded_keys = fold_cache(cache_keys, keep_flags, drop_weight)
    folded_values = fold_cache(cache_values, keep_flags, drop_weight)
    folded_bias = jnp.log((BLOCK - kept_count).astype(jnp.float32)).astype(jnp.bfloat16)
    packed_keys = jnp.zeros((slot_count, D), jnp.bfloat16).at[row_slot].set(cache_keys, mode='drop').at[fold_slot].set(folded_keys)
    packed_values = jnp.zeros((slot_count, D), jnp.bfloat16).at[row_slot].set(cache_values, mode='drop').at[fold_slot].set(folded_values)
    packed_bias = jnp.zeros((slot_count,), jnp.bfloat16).at[fold_slot].set(folded_bias)
    row_request = jnp.repeat(block_request, BLOCK)
    packed_request = jnp.full((slot_count,), -1, jnp.int32).at[row_slot].set(row_request, mode='drop').at[fold_slot].set(block_request)
    score_scale = 1.0 / jnp.sqrt(jnp.float32(HD))
    request_index = jnp.arange(REQS, dtype=jnp.int32)
    member = packed_request[None, :] == request_index[:, None]
    bias_row = packed_bias.astype(jnp.float32)[None, :]
    outputs = []
    for head_index in range(HEADS):
        lower = head_index * HD
        head_query = queries[:, lower:lower + HD]
        head_keys = packed_keys[:, lower:lower + HD]
        head_values = packed_values[:, lower:lower + HD]
        scores = jnp.dot(head_query, head_keys.T, preferred_element_type=jnp.float32) * score_scale + bias_row
        scores = jnp.where(member, scores, jnp.float32(-1e+30))
        own_score = lax.optimization_barrier(jnp.sum(head_query.astype(jnp.float32) * new_keys[:, lower:lower + HD].astype(jnp.float32), axis=1)) * score_scale
        peak = jnp.maximum(lax.optimization_barrier(jnp.max(scores, axis=1)), own_score)
        probs = jnp.where(member, jnp.exp(scores - peak[:, None]), jnp.float32(0.0))
        own_prob = jnp.exp(own_score - peak)
        total = lax.optimization_barrier(jnp.sum(probs, axis=1)) + own_prob
        weighted = jnp.dot(probs.astype(jnp.bfloat16), head_values, preferred_element_type=jnp.float32)
        weighted = weighted + own_prob[:, None] * new_values[:, lower:lower + HD].astype(jnp.float32)
        outputs.append(weighted / total[:, None])
    attention = jnp.concatenate(outputs, axis=1).astype(jnp.bfloat16)
    layer_output = jnp.dot(attention, out_weight, preferred_element_type=jnp.float32).astype(jnp.bfloat16)
    return (packed_keys, packed_values, packed_bias, packed_request, layer_output)
```

```python
import jax
import jax.numpy as jnp
from jax import lax
from jax.experimental import pallas as pl
from jax.experimental.pallas import tpu as pltpu
from jax.sharding import PartitionSpec as P

MESH = pl.DeviceIdType.MESH
F32, BF16, I32 = jnp.float32, jnp.bfloat16, jnp.int32

N = 64
TP = 8
HD = 256
BLOCK = 128
NB = 16
ROWS = 2048
REQS = 48
K_DEV = 1040
SLAB = 16
MAIN = N * SLAB
TILE = 208
TILES = K_DEV // TILE
NEG = -1e30


def iota(shape, dim):
    return lax.broadcasted_iota(I32, shape, dim)


def entry_of(t):
    return jnp.where(t < MAIN, (t & (SLAB - 1)) * N + (t >> 4), t)


def pack_kernel(
    k_ref, v_ref, keep_ref, w_ref, req_ref, q_ref, grp, counts, rsend, part
):
    me = lax.axis_index("seq")
    keep = keep_ref[...]
    keepf = keep.astype(F32)
    upper = (iota((BLOCK, BLOCK), 0) < iota((BLOCK, BLOCK), 1)).astype(BF16)
    within = jnp.dot(keepf.astype(BF16), upper, preferred_element_type=F32)
    kept_col = jnp.sum(keepf, axis=1, keepdims=True)
    size_col = kept_col + 1.0
    eye = iota((NB, BLOCK), 0) == iota((NB, BLOCK), 1)
    size_row = jnp.sum(jnp.where(eye, size_col, 0.0), axis=0, keepdims=True)
    base_col = jnp.sum(
        jnp.where(iota((NB, BLOCK), 1) < iota((NB, BLOCK), 0), size_row, 0.0), axis=1, keepdims=True
    )
    fold_col = base_col + kept_col
    counts[...] = size_row.astype(I32)
    entry = jnp.where(keep == 1, base_col + within, fold_col).astype(I32)
    tgt_in = jnp.where(entry < MAIN, ((entry & (N - 1)) << 4) | (entry >> 6), entry)
    dropped = w_ref[...] * (1 - keep)
    val_in = jnp.where(keep == 1, 1, dropped).astype(F32)
    denom_col = jnp.sum(dropped.astype(F32), axis=1, keepdims=True)
    inv_row = jnp.sum(jnp.where(eye, 1.0 / denom_col, 0.0), axis=0, keepdims=True)
    fold_row = jnp.sum(jnp.where(eye, fold_col, 0.0), axis=0, keepdims=True).astype(I32)
    fold_row = jnp.where(iota((1, BLOCK), 1) < NB, fold_row, -1)

    def group(j, _):
        start = pl.multiple_of(j * TILE, 16)
        t = iota((TILE, BLOCK), 0) + start
        pieces = [
            jnp.where(t == tgt_in[b : b + 1, :], val_in[b : b + 1, :], 0.0).astype(BF16)
            for b in range(NB)
        ]
        sel = jnp.concatenate(pieces, axis=1)
        is_fold = entry_of(t) == fold_row
        scale = jnp.sum(jnp.where(is_fold, inv_row, 0.0), axis=1, keepdims=True)
        scale = jnp.where(scale > 0.0, scale, 1.0)
        kk = jnp.dot(sel, k_ref[...], preferred_element_type=F32)
        vv = jnp.dot(sel, v_ref[...], preferred_element_type=F32)
        grp[pl.ds(start, TILE), 0:HD] = (kk * scale).astype(BF16)
        grp[pl.ds(start, TILE), HD : 2 * HD] = (vv * scale).astype(BF16)
        return 0

    lax.fori_loop(0, TILES, group, 0)

    spread = spread_rows()
    q64 = jnp.dot(spread, q_ref[...], preferred_element_type=F32)
    srow = iota((N, BLOCK), 0)
    lane = iota((N, BLOCK), 1)
    used = (srow & 7) < 6
    starts, ends = request_blocks(req_ref)
    gblock = (lane + me * NB).astype(F32)
    low = jnp.sum(jnp.where(gblock < starts, size_row, 0.0), axis=1, keepdims=True)
    high = jnp.sum(jnp.where((gblock < ends) & used, size_row, 0.0), axis=1, keepdims=True)
    log_col = jnp.log(float(BLOCK) - kept_col).astype(BF16).astype(F32)
    e_row = entry_of(iota((1, K_DEV), 1)).astype(F32)
    bias_row = jnp.sum(
        jnp.where(jnp.broadcast_to(e_row, (NB, K_DEV)) == fold_col, log_col, 0.0), axis=0, keepdims=True
    )
    scores = lax.dot_general(
        q64.astype(BF16), grp[:, 0:HD], (((1,), (1,)), ((), ())), preferred_element_type=F32
    )
    scores = scores * (1.0 / 16.0) + bias_row
    member = (e_row >= low) & (e_row < high)
    scores = jnp.where(member, scores, NEG)
    peak = jnp.max(scores, axis=1, keepdims=True)
    probs = jnp.where(member, jnp.exp(scores - peak), 0.0)
    total = jnp.sum(probs, axis=1, keepdims=True)
    part[:, 0:HD] = jnp.dot(probs.astype(BF16), grp[:, HD : 2 * HD], preferred_element_type=F32)
    part[:, HD : HD + 128] = jnp.broadcast_to(peak, (N, 128))
    part[:, HD + 128 : HD + 256] = jnp.broadcast_to(total, (N, 128))

    def fill_part(s, _):
        rsend[s] = part[pl.ds(s, 1), :]
        return 0

    lax.fori_loop(0, N, fill_part, 0)


def spread_rows():
    row, req = iota((N, REQS), 0), iota((N, REQS), 1)
    return ((6 * (row >> 3) + (row & 7) == req) & ((row & 7) < 6)).astype(BF16)


def request_blocks(req_ref):
    srow = iota((N, BLOCK), 0)
    lane = iota((N, BLOCK), 1)
    rid = 6 * (srow >> 3) + (srow & 7)
    req_row = req_ref[...].astype(F32)
    ends = jnp.sum(jnp.where(lane <= rid, req_row, 0.0), axis=1, keepdims=True)
    starts = jnp.sum(jnp.where(lane < rid, req_row, 0.0), axis=1, keepdims=True)
    return starts, ends


def turn_kernel(counts, grp, rrecv, q_ref, nk_ref, nv_ref, send, xsend, gsend, xf):
    me = lax.axis_index("seq")

    def sum_before(s, carry):
        return carry + jnp.where(s < me, counts[s], 0)

    before = lax.fori_loop(0, N, sum_before, jnp.zeros((1, BLOCK), I32))
    offset = jnp.sum(before)
    xf[...] = grp[MAIN:K_DEV, :].astype(F32)

    def turn(p, _):
        c = (p - offset) & (N - 1)
        send[p] = grp[pl.ds(pl.multiple_of(c * SLAB, SLAB), SLAB), :]
        row = xf[pl.ds(c & 15, 1), :]
        xsend[p] = jnp.concatenate([row[:, 0:HD], row[:, HD : 2 * HD]], axis=0).astype(BF16)
        return 0

    lax.fori_loop(0, N, turn, 0)

    mine = ((6 * (me >> 3) + (me & 7) == iota((8, REQS), 1)) & ((me & 7) < 6)).astype(BF16)
    qr = jnp.dot(mine, q_ref[...], preferred_element_type=F32)
    kr = jnp.dot(mine, nk_ref[...], preferred_element_type=F32)
    nv = jnp.dot(mine, nv_ref[...], preferred_element_type=F32)[0:1, :]
    own = jnp.sum(qr * kr, axis=1, keepdims=True)[0:1, :] * (1.0 / 16.0)
    own = jnp.broadcast_to(own, (1, 128))

    def top(i, carry):
        return jnp.maximum(carry, rrecv[i][:, HD : HD + 128])

    peak = lax.fori_loop(0, N, top, own)

    def merge(i, carry):
        tot, wsum = carry
        row = rrecv[i]
        w = jnp.exp(row[:, HD : HD + 128] - peak)
        tot = tot + w * row[:, HD + 128 : HD + 256]
        wsum = wsum + jnp.concatenate([w, w], axis=1) * row[:, 0:HD]
        return tot, wsum

    own_p = jnp.exp(own - peak)
    first = (own_p, jnp.concatenate([own_p, own_p], axis=1) * nv)
    tot, wsum = lax.fori_loop(0, N, merge, first, unroll=8)
    gsend[...] = (wsum / jnp.concatenate([tot, tot], axis=1)).astype(BF16).astype(F32)


def project_kernel(grecv, ow_ref, tsend, a2):
    def fill_rows(s, _):
        a2[pl.ds(s, 1), :] = grecv[s]
        return 0

    lax.fori_loop(0, N, fill_rows, 0)
    wide = jnp.dot(a2[...].astype(BF16), ow_ref[...], preferred_element_type=F32)
    for p in range(TP):
        tsend[p] = wide[8 * p : 8 * p + 8, :]


def place_kernel(counts, recv, xrecv, req_ref, pk_ref, pv_ref, pb_ref, pr_ref, c2, x2, tgt):
    me = lax.axis_index("seq")
    srow = iota((N, BLOCK), 0)
    lane = iota((N, BLOCK), 1)
    _, ends = request_blocks(req_ref)

    def fill_counts(s, _):
        c2[pl.ds(s, 1), :] = counts[s]
        return 0

    lax.fori_loop(0, N, fill_counts, 0)
    sizes = c2[...].astype(F32)
    sizes16 = sizes.astype(BF16)
    n_col = jnp.sum(sizes, axis=1, keepdims=True)
    before64 = (iota((N, N), 1) < iota((N, N), 0)).astype(BF16)
    off_col = jnp.sum(jnp.dot(before64, sizes16, preferred_element_type=F32), axis=1, keepdims=True)
    upto = (iota((BLOCK, BLOCK), 0) <= iota((BLOCK, BLOCK), 1)).astype(BF16)
    block_end = off_col + jnp.dot(sizes16, upto, preferred_element_type=F32)
    drops = jnp.where(lane < NB, float(BLOCK + 1) - sizes, 1.0)
    logs = jnp.log(drops).astype(BF16).astype(F32)
    j_row = (iota((1, K_DEV), 1) * N + me).astype(F32)
    bias_out = jnp.zeros((N, K_DEV), F32)
    for b in range(NB):
        hit = (block_end[:, b : b + 1] - 1.0) == j_row
        bias_out = jnp.where(hit, logs[:, b : b + 1], bias_out)
    pb_ref[...] = jnp.sum(bias_out, axis=0, keepdims=True).astype(BF16)
    last = ends.astype(I32) - 1
    pick = (iota((N, N), 1) == (last >> 4)).astype(F32)
    picked = jnp.dot(pick, block_end, preferred_element_type=F32, precision=lax.Precision.HIGHEST)
    req_end = jnp.sum(jnp.where(lane == (last & 15), picked, 0.0), axis=1, keepdims=True)
    past = ((req_end <= j_row) & ((iota((N, K_DEV), 0) & 7) < 6)).astype(F32)
    owner = jnp.sum(past, axis=0, keepdims=True)
    every = jnp.sum(n_col, axis=0, keepdims=True)
    pr_ref[...] = jnp.where(j_row < every, owner, -1.0).astype(I32)

    off_i = off_col.astype(I32)
    c_col = (me - off_i) & (N - 1)
    k0_col = ((off_i + c_col) >> 6).astype(F32)
    lim_col = n_col - c_col.astype(F32)
    col = iota((N, MAIN), 1)
    is_src = iota((N, MAIN), 0) == (col >> 4)
    k0 = jnp.sum(jnp.where(is_src, k0_col, 0.0), axis=0, keepdims=True)
    lim = jnp.sum(jnp.where(is_src, lim_col, 0.0), axis=0, keepdims=True)
    q = (col[0:1, :] & (SLAB - 1)).astype(F32)
    tgt[...] = jnp.where(q * N < lim, k0 + q, -1.0).astype(I32)
    is_src = srow == lane
    k0 = jnp.sum(jnp.where(is_src, k0_col, 0.0), axis=0, keepdims=True)
    lim = jnp.sum(jnp.where(is_src, lim_col, 0.0), axis=0, keepdims=True)
    xtgt = jnp.where(lim > float(MAIN), k0 + float(SLAB), -1.0).astype(I32)
    x2[...] = jnp.zeros(x2.shape, F32)

    def fill_extra(i, _):
        pair = xrecv[i].astype(F32)
        x2[pl.ds(i, 1), 0:HD] = pair[0:1, :]
        x2[pl.ds(i, 1), HD : 2 * HD] = pair[1:2, :]
        return 0

    lax.fori_loop(0, N, fill_extra, 0)

    def place(j, _):
        start = pl.multiple_of(j * TILE, 16)
        sel = jnp.where(iota((TILE, MAIN), 0) + start == tgt[...], 1.0, 0.0).astype(BF16)
        xsel = jnp.where(iota((TILE, BLOCK), 0) + start == xtgt, 1.0, 0.0).astype(BF16)
        rows = recv[...].reshape(MAIN, 2 * HD)
        got = jnp.dot(sel, rows, preferred_element_type=F32)
        got = got + jnp.dot(xsel, x2[...].astype(BF16), preferred_element_type=F32)
        pk_ref[pl.ds(start, TILE), :] = got[:, 0:HD].astype(BF16)
        pv_ref[pl.ds(start, TILE), :] = got[:, HD : 2 * HD].astype(BF16)
        return 0

    lax.fori_loop(0, TILES, place, 0)


def exchange_counts(counts, rsend):
    counts = lax.all_gather(counts, "seq", axis=0, tiled=False)
    return counts, lax.all_to_all(rsend, "seq", split_axis=0, concat_axis=0, tiled=True)


def exchange_main(send, xsend, gsend):
    recv = lax.all_to_all(send, "seq", split_axis=0, concat_axis=0, tiled=True)
    xrecv = lax.all_to_all(xsend, "seq", split_axis=0, concat_axis=0, tiled=True)
    return recv, xrecv, lax.all_gather(gsend, "seq", axis=0, tiled=False)


def exchange_tp(tsend):
    mine = lax.psum_scatter(tsend, "tp", scatter_dimension=0, tiled=False)
    return mine[0:6, 0:32].astype(BF16)


def local(body, name, outs, scratch, *args):
    vmem = pl.BlockSpec(memory_space=pltpu.VMEM)
    return pl.pallas_call(
        body,
        name=name,
        out_shape=tuple(jax.ShapeDtypeStruct(s, d) for s, d in outs),
        in_specs=[vmem] * len(args),
        out_specs=(vmem,) * len(outs),
        scratch_shapes=[pltpu.VMEM(s, d) for s, d in scratch],
        compiler_params=pltpu.CompilerParams(vmem_limit_bytes=40 << 20),
    )(*args)


def on_device(ck, cv, keep, w, req, q, nk, nv, ow):
    keep2 = keep.reshape(NB, BLOCK)
    w2 = w.reshape(NB, BLOCK)
    req2 = jnp.pad(req, (0, BLOCK - REQS)).reshape(1, BLOCK)
    ow2 = jnp.pad(ow, ((0, 0), (0, 128 - ow.shape[1])))
    grp, counts, rsend = local(
        pack_kernel, "pack",
        [((K_DEV, 2 * HD), BF16), ((1, BLOCK), I32), ((N, 1, 2 * HD), F32)],
        [((N, 2 * HD), F32)],
        ck, cv, keep2, w2, req2, q,
    )
    counts, rrecv = exchange_counts(counts, rsend)
    send, xsend, gsend = local(
        turn_kernel, "turn",
        [((N, SLAB, 2 * HD), BF16), ((N, 2, HD), BF16), ((1, HD), F32)],
        [((16, 2 * HD), F32)],
        counts, grp, rrecv, q, nk, nv,
    )
    recv, xrecv, grecv = exchange_main(send, xsend, gsend)
    (tsend,) = local(project_kernel, "project", [((TP, 8, 128), F32)], [((N, HD), F32)], grecv, ow2)
    lo = exchange_tp(tsend)
    pk, pv, pb, pr = local(
        place_kernel, "place",
        [((K_DEV, HD), BF16), ((K_DEV, HD), BF16), ((1, K_DEV), BF16), ((1, K_DEV), I32)],
        [((N, BLOCK), I32), ((BLOCK, 2 * HD), F32), ((1, MAIN), I32)],
        counts, recv, xrecv, req2,
    )
    return pk, pv, pb.reshape(K_DEV), pr.reshape(K_DEV), lo


def solution(mesh):
    in_specs = (
        P("seq", "tp"), P("seq", "tp"), P("seq"), P("seq"), P(),
        P(None, "tp"), P(None, "tp"), P(None, "tp"), P("tp", "seq"),
    )
    out_specs = (P("seq", "tp"), P("seq", "tp"), P("seq"), P("seq"), P("tp", "seq"))
    return jax.shard_map(on_device, mesh=mesh, in_specs=in_specs, out_specs=out_specs, check_vma=False)
```

```python
import jax
import jax.numpy as jnp
from jax import lax
from jax.experimental import pallas as pl
from jax.experimental.pallas import tpu as pltpu
from jax.sharding import PartitionSpec as P

MESH = pl.DeviceIdType.MESH
F32, BF16, I32 = jnp.float32, jnp.bfloat16, jnp.int32

N = 64
TP = 8
HD = 256
BLOCK = 128
NB = 16
ROWS = 2048
REQS = 48
K_DEV = 1040
SLAB = 16
MAIN = N * SLAB
TILE = 208
TILES = K_DEV // TILE
NEG = -1e30


def iota(shape, dim):
    return lax.broadcasted_iota(I32, shape, dim)


def entry_of(t):
    return jnp.where(t < MAIN, (t & (SLAB - 1)) * N + (t >> 4), t)


def pack_kernel(
    k_ref, v_ref, keep_ref, w_ref, req_ref, q_ref, grp, counts, rsend, part
):
    me = lax.axis_index("seq")
    keep = keep_ref[...]
    keepf = keep.astype(F32)
    upper = (iota((BLOCK, BLOCK), 0) < iota((BLOCK, BLOCK), 1)).astype(BF16)
    within = jnp.dot(keepf.astype(BF16), upper, preferred_element_type=F32)
    kept_col = jnp.sum(keepf, axis=1, keepdims=True)
    size_col = kept_col + 1.0
    eye = iota((NB, BLOCK), 0) == iota((NB, BLOCK), 1)
    size_row = jnp.sum(jnp.where(eye, size_col, 0.0), axis=0, keepdims=True)
    base_col = jnp.sum(
        jnp.where(iota((NB, BLOCK), 1) < iota((NB, BLOCK), 0), size_row, 0.0), axis=1, keepdims=True
    )
    fold_col = base_col + kept_col
    counts[...] = size_row.astype(I32)
    entry = jnp.where(keep == 1, base_col + within, fold_col).astype(I32)
    tgt_in = jnp.where(entry < MAIN, ((entry & (N - 1)) << 4) | (entry >> 6), entry)
    dropped = w_ref[...] * (1 - keep)
    val_in = jnp.where(keep == 1, 1, dropped).astype(F32)
    denom_col = jnp.sum(dropped.astype(F32), axis=1, keepdims=True)
    inv_row = jnp.sum(jnp.where(eye, 1.0 / denom_col, 0.0), axis=0, keepdims=True)
    fold_row = jnp.sum(jnp.where(eye, fold_col, 0.0), axis=0, keepdims=True).astype(I32)
    fold_row = jnp.where(iota((1, BLOCK), 1) < NB, fold_row, -1)

    def group(j, _):
        start = pl.multiple_of(j * TILE, 16)
        t = iota((TILE, BLOCK), 0) + start
        pieces = [
            jnp.where(t == tgt_in[b : b + 1, :], val_in[b : b + 1, :], 0.0).astype(BF16)
            for b in range(NB)
        ]
        sel = jnp.concatenate(pieces, axis=1)
        is_fold = entry_of(t) == fold_row
        scale = jnp.sum(jnp.where(is_fold, inv_row, 0.0), axis=1, keepdims=True)
        scale = jnp.where(scale > 0.0, scale, 1.0)
        kk = jnp.dot(sel, k_ref[...], preferred_element_type=F32)
        vv = jnp.dot(sel, v_ref[...], preferred_element_type=F32)
        grp[pl.ds(start, TILE), 0:HD] = (kk * scale).astype(BF16)
        grp[pl.ds(start, TILE), HD : 2 * HD] = (vv * scale).astype(BF16)
        return 0

    lax.fori_loop(0, TILES, group, 0)

    spread = spread_rows()
    q64 = jnp.dot(spread, q_ref[...], preferred_element_type=F32)
    srow = iota((N, BLOCK), 0)
    lane = iota((N, BLOCK), 1)
    used = (srow & 7) < 6
    starts, ends = request_blocks(req_ref)
    gblock = (lane + me * NB).astype(F32)
    low = jnp.sum(jnp.where(gblock < starts, size_row, 0.0), axis=1, keepdims=True)
    high = jnp.sum(jnp.where((gblock < ends) & used, size_row, 0.0), axis=1, keepdims=True)
    log_col = jnp.log(float(BLOCK) - kept_col).astype(BF16).astype(F32)
    e_row = entry_of(iota((1, K_DEV), 1)).astype(F32)
    bias_row = jnp.sum(
        jnp.where(jnp.broadcast_to(e_row, (NB, K_DEV)) == fold_col, log_col, 0.0), axis=0, keepdims=True
    )
    scores = lax.dot_general(
        q64.astype(BF16), grp[:, 0:HD], (((1,), (1,)), ((), ())), preferred_element_type=F32
    )
    scores = scores * (1.0 / 16.0) + bias_row
    member = (e_row >= low) & (e_row < high)
    scores = jnp.where(member, scores, NEG)
    peak = jnp.max(scores, axis=1, keepdims=True)
    probs = jnp.where(member, jnp.exp(scores - peak), 0.0)
    total = jnp.sum(probs, axis=1, keepdims=True)
    part[:, 0:HD] = jnp.dot(probs.astype(BF16), grp[:, HD : 2 * HD], preferred_element_type=F32)
    part[:, HD : HD + 128] = jnp.broadcast_to(peak, (N, 128))
    part[:, HD + 128 : HD + 256] = jnp.broadcast_to(total, (N, 128))

    def fill_part(s, _):
        rsend[s] = part[pl.ds(s, 1), :]
        return 0

    lax.fori_loop(0, N, fill_part, 0)


def spread_rows():
    row, req = iota((N, REQS), 0), iota((N, REQS), 1)
    return ((6 * (row >> 3) + (row & 7) == req) & ((row & 7) < 6)).astype(BF16)


def request_blocks(req_ref):
    srow = iota((N, BLOCK), 0)
    lane = iota((N, BLOCK), 1)
    rid = 6 * (srow >> 3) + (srow & 7)
    req_row = req_ref[...].astype(F32)
    ends = jnp.sum(jnp.where(lane <= rid, req_row, 0.0), axis=1, keepdims=True)
    starts = jnp.sum(jnp.where(lane < rid, req_row, 0.0), axis=1, keepdims=True)
    return starts, ends


def turn_kernel(counts, grp, rrecv, q_ref, nk_ref, nv_ref, send, xsend, gsend, xf):
    me = lax.axis_index("seq")

    def sum_before(s, carry):
        return carry + jnp.where(s < me, counts[s], 0)

    before = lax.fori_loop(0, N, sum_before, jnp.zeros((1, BLOCK), I32))
    offset = jnp.sum(before)
    xf[...] = grp[MAIN:K_DEV, :].astype(F32)

    def turn(p, _):
        c = (p - offset) & (N - 1)
        send[p] = grp[pl.ds(pl.multiple_of(c * SLAB, SLAB), SLAB), :]
        row = xf[pl.ds(c & 15, 1), :]
        xsend[p] = jnp.concatenate([row[:, 0:HD], row[:, HD : 2 * HD]], axis=0).astype(BF16)
        return 0

    lax.fori_loop(0, N, turn, 0)

    mine = ((6 * (me >> 3) + (me & 7) == iota((8, REQS), 1)) & ((me & 7) < 6)).astype(BF16)
    qr = jnp.dot(mine, q_ref[...], preferred_element_type=F32)
    kr = jnp.dot(mine, nk_ref[...], preferred_element_type=F32)
    nv = jnp.dot(mine, nv_ref[...], preferred_element_type=F32)[0:1, :]
    own = jnp.sum(qr * kr, axis=1, keepdims=True)[0:1, :] * (1.0 / 16.0)
    own = jnp.broadcast_to(own, (1, 128))

    def top(i, carry):
        return jnp.maximum(carry, rrecv[i][:, HD : HD + 128])

    peak = lax.fori_loop(0, N, top, own)

    def merge(i, carry):
        tot, wsum = carry
        row = rrecv[i]
        w = jnp.exp(row[:, HD : HD + 128] - peak)
        tot = tot + w * row[:, HD + 128 : HD + 256]
        wsum = wsum + jnp.concatenate([w, w], axis=1) * row[:, 0:HD]
        return tot, wsum

    own_p = jnp.exp(own - peak)
    first = (own_p, jnp.concatenate([own_p, own_p], axis=1) * nv)
    tot, wsum = lax.fori_loop(0, N, merge, first, unroll=8)
    gsend[...] = (wsum / jnp.concatenate([tot, tot], axis=1)).astype(BF16).astype(F32)


def project_kernel(grecv, ow_ref, tsend, a2):
    def fill_rows(s, _):
        a2[pl.ds(s, 1), :] = grecv[s]
        return 0

    lax.fori_loop(0, N, fill_rows, 0)
    wide = jnp.dot(a2[...].astype(BF16), ow_ref[...], preferred_element_type=F32)
    for p in range(TP):
        tsend[p] = wide[8 * p : 8 * p + 8, :]


def place_kernel(counts, recv, xrecv, req_ref, pk_ref, pv_ref, pb_ref, pr_ref, c2, x2, tgt):
    me = lax.axis_index("seq")
    srow = iota((N, BLOCK), 0)
    lane = iota((N, BLOCK), 1)
    _, ends = request_blocks(req_ref)

    def fill_counts(s, _):
        c2[pl.ds(s, 1), :] = counts[s]
        return 0

    lax.fori_loop(0, N, fill_counts, 0)
    sizes = c2[...].astype(F32)
    sizes16 = sizes.astype(BF16)
    n_col = jnp.sum(sizes, axis=1, keepdims=True)
    before64 = (iota((N, N), 1) < iota((N, N), 0)).astype(BF16)
    off_col = jnp.sum(jnp.dot(before64, sizes16, preferred_element_type=F32), axis=1, keepdims=True)
    upto = (iota((BLOCK, BLOCK), 0) <= iota((BLOCK, BLOCK), 1)).astype(BF16)
    block_end = off_col + jnp.dot(sizes16, upto, preferred_element_type=F32)
    drops = jnp.where(lane < NB, float(BLOCK + 1) - sizes, 1.0)
    logs = jnp.log(drops).astype(BF16).astype(F32)
    j_row = (iota((1, K_DEV), 1) * N + me).astype(F32)
    bias_out = jnp.zeros((N, K_DEV), F32)
    for b in range(NB):
        hit = (block_end[:, b : b + 1] - 1.0) == j_row
        bias_out = jnp.where(hit, logs[:, b : b + 1], bias_out)
    pb_ref[...] = jnp.sum(bias_out, axis=0, keepdims=True).astype(BF16)
    last = ends.astype(I32) - 1
    pick = (iota((N, N), 1) == (last >> 4)).astype(F32)
    picked = jnp.dot(pick, block_end, preferred_element_type=F32, precision=lax.Precision.HIGHEST)
    req_end = jnp.sum(jnp.where(lane == (last & 15), picked, 0.0), axis=1, keepdims=True)
    past = ((req_end <= j_row) & ((iota((N, K_DEV), 0) & 7) < 6)).astype(F32)
    owner = jnp.sum(past, axis=0, keepdims=True)
    every = jnp.sum(n_col, axis=0, keepdims=True)
    pr_ref[...] = jnp.where(j_row < every, owner, -1.0).astype(I32)

    off_i = off_col.astype(I32)
    c_col = (me - off_i) & (N - 1)
    k0_col = ((off_i + c_col) >> 6).astype(F32)
    lim_col = n_col - c_col.astype(F32)
    col = iota((N, MAIN), 1)
    is_src = iota((N, MAIN), 0) == (col >> 4)
    k0 = jnp.sum(jnp.where(is_src, k0_col, 0.0), axis=0, keepdims=True)
    lim = jnp.sum(jnp.where(is_src, lim_col, 0.0), axis=0, keepdims=True)
    q = (col[0:1, :] & (SLAB - 1)).astype(F32)
    tgt[...] = jnp.where(q * N < lim, k0 + q, -1.0).astype(I32)
    is_src = srow == lane
    k0 = jnp.sum(jnp.where(is_src, k0_col, 0.0), axis=0, keepdims=True)
    lim = jnp.sum(jnp.where(is_src, lim_col, 0.0), axis=0, keepdims=True)
    xtgt = jnp.where(lim > float(MAIN), k0 + float(SLAB), -1.0).astype(I32)
    x2[...] = jnp.zeros(x2.shape, F32)

    def fill_extra(i, _):
        pair = xrecv[i].astype(F32)
        x2[pl.ds(i, 1), 0:HD] = pair[0:1, :]
        x2[pl.ds(i, 1), HD : 2 * HD] = pair[1:2, :]
        return 0

    lax.fori_loop(0, N, fill_extra, 0)

    def place(j, _):
        start = pl.multiple_of(j * TILE, 16)
        sel = jnp.where(iota((TILE, MAIN), 0) + start == tgt[...], 1.0, 0.0).astype(BF16)
        xsel = jnp.where(iota((TILE, BLOCK), 0) + start == xtgt, 1.0, 0.0).astype(BF16)
        rows = recv[...].reshape(MAIN, 2 * HD)
        got = jnp.dot(sel, rows, preferred_element_type=F32)
        got = got + jnp.dot(xsel, x2[...].astype(BF16), preferred_element_type=F32)
        pk_ref[pl.ds(start, TILE), :] = got[:, 0:HD].astype(BF16)
        pv_ref[pl.ds(start, TILE), :] = got[:, HD : 2 * HD].astype(BF16)
        return 0

    lax.fori_loop(0, TILES, place, 0)


def remote(body, name, cid, outs, *args):
    vmem = pl.BlockSpec(memory_space=pltpu.VMEM)
    return pl.pallas_call(
        body,
        name=name,
        out_shape=tuple(jax.ShapeDtypeStruct(s, d) for s, d in outs),
        in_specs=[vmem] * len(args),
        out_specs=(vmem,) * len(outs),
        scratch_shapes=[pltpu.SemaphoreType.DMA] * (2 * len(outs) + 1),
        compiler_params=pltpu.CompilerParams(
            collective_id=cid, has_side_effects=True, vmem_limit_bytes=40 << 20
        ),
    )(*args)


def swap(axis, count, moves, local_sem):
    me = lax.axis_index(axis)

    barrier = pltpu.get_barrier_semaphore()

    def greet(i, _):
        p = lax.rem(me + 1 + i, count)
        pl.semaphore_signal(barrier, inc=1, device_id={axis: p}, device_id_type=MESH)
        return 0

    lax.fori_loop(0, count - 1, greet, 0)
    for src, dst, whole, _, _ in moves:
        copy = pltpu.make_async_copy(src if whole else src.at[me], dst.at[me], local_sem)
        copy.start()
        copy.wait()
    pl.semaphore_wait(barrier, count - 1)

    def go(i, _):
        p = lax.rem(me + 1 + i, count)
        for src, dst, whole, s_sem, r_sem in moves:
            pltpu.make_async_remote_copy(
                src if whole else src.at[p], dst.at[me], s_sem, r_sem,
                device_id={axis: p}, device_id_type=MESH,
            ).start()
        return 0

    lax.fori_loop(0, count - 1, go, 0)
    for _, dst, _, s_sem, r_sem in moves:
        many = dst.at[pl.ds(0, count - 1)]
        wait = pltpu.make_async_remote_copy(
            many, many, s_sem, r_sem, device_id={axis: lax.rem(me + 1, count)}, device_id_type=MESH
        )
        wait.wait_recv()
        wait.wait_send()


def counts_kernel(counts, rsend, call, rrecv, s0, r0, s1, r1, sem):
    swap("seq", N, [(counts, call, True, s0, r0), (rsend, rrecv, False, s1, r1)], sem)


def main_kernel(send, xsend, gsend, recv, xrecv, grecv, s0, r0, s1, r1, s2, r2, sem):
    swap(
        "seq", N,
        [(gsend, grecv, True, s2, r2), (send, recv, False, s0, r0), (xsend, xrecv, False, s1, r1)],
        sem,
    )


def tp_kernel(tsend, trecv, s0, r0, sem):
    swap("tp", TP, [(tsend, trecv, False, s0, r0)], sem)


def exchange_counts(counts, rsend):
    return remote(
        counts_kernel, "swap_counts", 0, [((N, 1, BLOCK), I32), ((N, 1, 2 * HD), F32)], counts, rsend
    )


def exchange_main(send, xsend, gsend):
    return remote(
        main_kernel, "swap_main", 1,
        [((N, SLAB, 2 * HD), BF16), ((N, 2, HD), BF16), ((N, 1, HD), F32)],
        send, xsend, gsend,
    )


def exchange_tp(tsend):
    (trecv,) = remote(tp_kernel, "swap_tp", 2, [((TP, 8, 128), F32)], tsend)
    return jnp.sum(trecv, axis=0)[0:6, 0:32].astype(BF16)


def local(body, name, outs, scratch, *args):
    vmem = pl.BlockSpec(memory_space=pltpu.VMEM)
    return pl.pallas_call(
        body,
        name=name,
        out_shape=tuple(jax.ShapeDtypeStruct(s, d) for s, d in outs),
        in_specs=[vmem] * len(args),
        out_specs=(vmem,) * len(outs),
        scratch_shapes=[pltpu.VMEM(s, d) for s, d in scratch],
        compiler_params=pltpu.CompilerParams(vmem_limit_bytes=40 << 20),
    )(*args)


def on_device(ck, cv, keep, w, req, q, nk, nv, ow):
    keep2 = keep.reshape(NB, BLOCK)
    w2 = w.reshape(NB, BLOCK)
    req2 = jnp.pad(req, (0, BLOCK - REQS)).reshape(1, BLOCK)
    ow2 = jnp.pad(ow, ((0, 0), (0, 128 - ow.shape[1])))
    grp, counts, rsend = local(
        pack_kernel, "pack",
        [((K_DEV, 2 * HD), BF16), ((1, BLOCK), I32), ((N, 1, 2 * HD), F32)],
        [((N, 2 * HD), F32)],
        ck, cv, keep2, w2, req2, q,
    )
    counts, rrecv = exchange_counts(counts, rsend)
    send, xsend, gsend = local(
        turn_kernel, "turn",
        [((N, SLAB, 2 * HD), BF16), ((N, 2, HD), BF16), ((1, HD), F32)],
        [((16, 2 * HD), F32)],
        counts, grp, rrecv, q, nk, nv,
    )
    recv, xrecv, grecv = exchange_main(send, xsend, gsend)
    (tsend,) = local(project_kernel, "project", [((TP, 8, 128), F32)], [((N, HD), F32)], grecv, ow2)
    lo = exchange_tp(tsend)
    pk, pv, pb, pr = local(
        place_kernel, "place",
        [((K_DEV, HD), BF16), ((K_DEV, HD), BF16), ((1, K_DEV), BF16), ((1, K_DEV), I32)],
        [((N, BLOCK), I32), ((BLOCK, 2 * HD), F32), ((1, MAIN), I32)],
        counts, recv, xrecv, req2,
    )
    return pk, pv, pb.reshape(K_DEV), pr.reshape(K_DEV), lo


def solution(mesh):
    in_specs = (
        P("seq", "tp"), P("seq", "tp"), P("seq"), P("seq"), P(),
        P(None, "tp"), P(None, "tp"), P(None, "tp"), P("tp", "seq"),
    )
    out_specs = (P("seq", "tp"), P("seq", "tp"), P("seq"), P("seq"), P("tp", "seq"))
    return jax.shard_map(on_device, mesh=mesh, in_specs=in_specs, out_specs=out_specs, check_vma=False)
```

```python
import jax
import jax.numpy as jnp
from jax import lax
from jax.experimental import pallas as pl
from jax.experimental.pallas import tpu as pltpu
from jax.sharding import PartitionSpec as P

MESH = pl.DeviceIdType.MESH
F32, BF16, I32 = jnp.float32, jnp.bfloat16, jnp.int32

N = 64
TP = 8
HD = 256
BLOCK = 128
NB = 16
ROWS = 2048
REQS = 48
K_DEV = 1040
SLAB = 16
MAIN = N * SLAB
TILE = 208
TILES = K_DEV // TILE
NEG = -1e30
FIRST, SECOND = 24, 44


def iota(shape, dim):
    return lax.broadcasted_iota(I32, shape, dim)


def entry_of(t):
    return jnp.where(t < MAIN, (t & (SLAB - 1)) * N + (t >> 4), t)


def pack_kernel(
    k_ref, v_ref, keep_ref, w_ref, req_ref, q_ref, nk_ref, nv_ref,
    twice, xtwice, counts, rsend, own_ref, grp, part, xf
):
    me = lax.axis_index("seq")
    keep = keep_ref[...]
    keepf = keep.astype(F32)
    upper = (iota((BLOCK, BLOCK), 0) < iota((BLOCK, BLOCK), 1)).astype(BF16)
    within = jnp.dot(keepf.astype(BF16), upper, preferred_element_type=F32)
    kept_col = jnp.sum(keepf, axis=1, keepdims=True)
    size_col = kept_col + 1.0
    eye = iota((NB, BLOCK), 0) == iota((NB, BLOCK), 1)
    size_row = jnp.sum(jnp.where(eye, size_col, 0.0), axis=0, keepdims=True)
    base_col = jnp.sum(
        jnp.where(iota((NB, BLOCK), 1) < iota((NB, BLOCK), 0), size_row, 0.0), axis=1, keepdims=True
    )
    fold_col = base_col + kept_col
    counts[...] = size_row.astype(I32)
    entry = jnp.where(keep == 1, base_col + within, fold_col).astype(I32)
    tgt_in = jnp.where(entry < MAIN, ((entry & (N - 1)) << 4) | (entry >> 6), entry)
    dropped = w_ref[...] * (1 - keep)
    val_in = jnp.where(keep == 1, 1, dropped).astype(F32)
    denom_col = jnp.sum(dropped.astype(F32), axis=1, keepdims=True)
    inv_row = jnp.sum(jnp.where(eye, 1.0 / denom_col, 0.0), axis=0, keepdims=True)
    fold_row = jnp.sum(jnp.where(eye, fold_col, 0.0), axis=0, keepdims=True).astype(I32)
    fold_row = jnp.where(iota((1, BLOCK), 1) < NB, fold_row, -1)

    def group(j, _):
        start = pl.multiple_of(j * TILE, 16)
        t = iota((TILE, BLOCK), 0) + start
        pieces = [
            jnp.where(t == tgt_in[b : b + 1, :], val_in[b : b + 1, :], 0.0).astype(BF16)
            for b in range(NB)
        ]
        sel = jnp.concatenate(pieces, axis=1)
        is_fold = entry_of(t) == fold_row
        scale = jnp.sum(jnp.where(is_fold, inv_row, 0.0), axis=1, keepdims=True)
        scale = jnp.where(scale > 0.0, scale, 1.0)
        kk = jnp.dot(sel, k_ref[...], preferred_element_type=F32)
        vv = jnp.dot(sel, v_ref[...], preferred_element_type=F32)
        grp[pl.ds(start, TILE), 0:HD] = (kk * scale).astype(BF16)
        grp[pl.ds(start, TILE), HD : 2 * HD] = (vv * scale).astype(BF16)
        return 0

    lax.fori_loop(0, TILES, group, 0)
    slabs = grp[0:MAIN, :].reshape(N, SLAB, 2 * HD)
    twice[0:N] = slabs
    twice[N : 2 * N] = slabs
    xf[...] = grp[MAIN:K_DEV, :].astype(F32)
    xtwice[...] = jnp.zeros(xtwice.shape, BF16)
    for c in range(K_DEV - MAIN):
        row = xf[c : c + 1, :]
        pair = jnp.concatenate([row[:, 0:HD], row[:, HD : 2 * HD]], axis=0).astype(BF16)
        xtwice[c] = pair
        xtwice[N + c] = pair

    spread = spread_rows()
    q64 = jnp.dot(spread, q_ref[...], preferred_element_type=F32)
    srow = iota((N, BLOCK), 0)
    lane = iota((N, BLOCK), 1)
    used = (srow & 7) < 6
    starts, ends = request_blocks(req_ref)
    gblock = (lane + me * NB).astype(F32)
    low = jnp.sum(jnp.where(gblock < starts, size_row, 0.0), axis=1, keepdims=True)
    high = jnp.sum(jnp.where((gblock < ends) & used, size_row, 0.0), axis=1, keepdims=True)
    log_col = jnp.log(float(BLOCK) - kept_col).astype(BF16).astype(F32)
    e_row = entry_of(iota((1, K_DEV), 1)).astype(F32)
    bias_row = jnp.sum(
        jnp.where(jnp.broadcast_to(e_row, (NB, K_DEV)) == fold_col, log_col, 0.0), axis=0, keepdims=True
    )
    scores = lax.dot_general(
        q64.astype(BF16), grp[:, 0:HD], (((1,), (1,)), ((), ())), preferred_element_type=F32
    )
    scores = scores * (1.0 / 16.0) + bias_row
    member = (e_row >= low) & (e_row < high)
    scores = jnp.where(member, scores, NEG)
    peak = jnp.max(scores, axis=1, keepdims=True)
    probs = jnp.where(member, jnp.exp(scores - peak), 0.0)
    total = jnp.sum(probs, axis=1, keepdims=True)
    part[:, 0:HD] = jnp.dot(probs.astype(BF16), grp[:, HD : 2 * HD], preferred_element_type=F32)
    part[:, HD : HD + 128] = jnp.broadcast_to(peak, (N, 128))
    part[:, HD + 128 : HD + 256] = jnp.broadcast_to(total, (N, 128))

    def fill_part(s, _):
        rsend[s] = part[pl.ds(s, 1), :]
        return 0

    lax.fori_loop(0, N, fill_part, 0, unroll=8)

    mine = ((6 * (me >> 3) + (me & 7) == iota((8, REQS), 1)) & ((me & 7) < 6)).astype(BF16)
    qr = jnp.dot(mine, q_ref[...], preferred_element_type=F32)
    kr = jnp.dot(mine, nk_ref[...], preferred_element_type=F32)
    nv = jnp.dot(mine, nv_ref[...], preferred_element_type=F32)[0:1, :]
    own = jnp.sum(qr * kr, axis=1, keepdims=True)[0:1, :] * (1.0 / 16.0)
    own_ref[:, 0:HD] = nv
    own_ref[:, HD : HD + 128] = jnp.broadcast_to(own, (1, 128))


def spread_rows():
    row, req = iota((N, REQS), 0), iota((N, REQS), 1)
    return ((6 * (row >> 3) + (row & 7) == req) & ((row & 7) < 6)).astype(BF16)


def request_blocks(req_ref):
    srow = iota((N, BLOCK), 0)
    lane = iota((N, BLOCK), 1)
    rid = 6 * (srow >> 3) + (srow & 7)
    req_row = req_ref[...].astype(F32)
    ends = jnp.sum(jnp.where(lane <= rid, req_row, 0.0), axis=1, keepdims=True)
    starts = jnp.sum(jnp.where(lane < rid, req_row, 0.0), axis=1, keepdims=True)
    return starts, ends


def place_kernel(counts, recv, xrecv, req_ref, pk_ref, pv_ref, pb_ref, pr_ref, c2, x2, tgt):
    me = lax.axis_index("seq")
    srow = iota((N, BLOCK), 0)
    lane = iota((N, BLOCK), 1)
    _, ends = request_blocks(req_ref)

    def fill_counts(s, _):
        c2[pl.ds(s, 1), :] = counts[s]
        return 0

    lax.fori_loop(0, N, fill_counts, 0)
    sizes = c2[...].astype(F32)
    sizes16 = sizes.astype(BF16)
    n_col = jnp.sum(sizes, axis=1, keepdims=True)
    before64 = (iota((N, N), 1) < iota((N, N), 0)).astype(BF16)
    off_col = jnp.sum(jnp.dot(before64, sizes16, preferred_element_type=F32), axis=1, keepdims=True)
    upto = (iota((BLOCK, BLOCK), 0) <= iota((BLOCK, BLOCK), 1)).astype(BF16)
    block_end = off_col + jnp.dot(sizes16, upto, preferred_element_type=F32)
    drops = jnp.where(lane < NB, float(BLOCK + 1) - sizes, 1.0)
    logs = jnp.log(drops).astype(BF16).astype(F32)
    j_row = (iota((1, K_DEV), 1) * N + me).astype(F32)
    bias_out = jnp.zeros((N, K_DEV), F32)
    for b in range(NB):
        hit = (block_end[:, b : b + 1] - 1.0) == j_row
        bias_out = jnp.where(hit, logs[:, b : b + 1], bias_out)
    pb_ref[...] = jnp.sum(bias_out, axis=0, keepdims=True).astype(BF16)
    last = ends.astype(I32) - 1
    pick = (iota((N, N), 1) == (last >> 4)).astype(F32)
    picked = jnp.dot(pick, block_end, preferred_element_type=F32, precision=lax.Precision.HIGHEST)
    req_end = jnp.sum(jnp.where(lane == (last & 15), picked, 0.0), axis=1, keepdims=True)
    past = ((req_end <= j_row) & ((iota((N, K_DEV), 0) & 7) < 6)).astype(F32)
    owner = jnp.sum(past, axis=0, keepdims=True)
    every = jnp.sum(n_col, axis=0, keepdims=True)
    pr_ref[...] = jnp.where(j_row < every, owner, -1.0).astype(I32)

    off_i = off_col.astype(I32)
    c_col = (me - off_i) & (N - 1)
    k0_col = ((off_i + c_col) >> 6).astype(F32)
    lim_col = n_col - c_col.astype(F32)
    col = iota((N, MAIN), 1)
    is_src = iota((N, MAIN), 0) == (col >> 4)
    k0 = jnp.sum(jnp.where(is_src, k0_col, 0.0), axis=0, keepdims=True)
    lim = jnp.sum(jnp.where(is_src, lim_col, 0.0), axis=0, keepdims=True)
    q = (col[0:1, :] & (SLAB - 1)).astype(F32)
    tgt[...] = jnp.where(q * N < lim, k0 + q, -1.0).astype(I32)
    is_src = srow == lane
    k0 = jnp.sum(jnp.where(is_src, k0_col, 0.0), axis=0, keepdims=True)
    lim = jnp.sum(jnp.where(is_src, lim_col, 0.0), axis=0, keepdims=True)
    xtgt = jnp.where(lim > float(MAIN), k0 + float(SLAB), -1.0).astype(I32)
    x2[...] = jnp.zeros(x2.shape, F32)

    def fill_extra(i, _):
        pair = xrecv[i].astype(F32)
        x2[pl.ds(i, 1), 0:HD] = pair[0:1, :]
        x2[pl.ds(i, 1), HD : 2 * HD] = pair[1:2, :]
        return 0

    lax.fori_loop(0, N, fill_extra, 0)

    def place(j, _):
        start = pl.multiple_of(j * TILE, 16)
        sel = jnp.where(iota((TILE, MAIN), 0) + start == tgt[...], 1.0, 0.0).astype(BF16)
        xsel = jnp.where(iota((TILE, BLOCK), 0) + start == xtgt, 1.0, 0.0).astype(BF16)
        rows = recv[...].reshape(MAIN, 2 * HD)
        got = jnp.dot(sel, rows, preferred_element_type=F32)
        got = got + jnp.dot(xsel, x2[...].astype(BF16), preferred_element_type=F32)
        pk_ref[pl.ds(start, TILE), :] = got[:, 0:HD].astype(BF16)
        pv_ref[pl.ds(start, TILE), :] = got[:, HD : 2 * HD].astype(BF16)
        return 0

    lax.fori_loop(0, TILES, place, 0)


def step_of(i):
    half = (i + 1) // 2
    return N // 2 + half * (1 - 2 * (i % 2))


def swap_kernel(
    counts, rsend, twice, xtwice, own_ref, ow_ref,
    call, recv, xrecv, lo_ref,
    send, xsend, rrecv, gsend, grecv, tsend, trecv,
    s_c, r_c, s_p, r_p, s_m, r_m, s_x, r_x, s_g, r_g, s_t, r_t,
):
    me = lax.axis_index("seq")
    mt = lax.axis_index("tp")

    def seq_copy(src, dst, s_sem, r_sem, p):
        return pltpu.make_async_remote_copy(
            src, dst, s_sem, r_sem, device_id={"seq": p}, device_id_type=MESH
        )

    def tp_copy(src, dst, p):
        return pltpu.make_async_remote_copy(
            src, dst, s_t, r_t, device_id={"tp": p}, device_id_type=MESH
        )

    def partner(i):
        return lax.rem(me + step_of(i), N)

    barrier = pltpu.get_barrier_semaphore()

    def greet(i, _):
        pl.semaphore_signal(barrier, inc=1, device_id={"seq": partner(i)}, device_id_type=MESH)
        return 0

    lax.fori_loop(0, N - 1, greet, 0)

    def greet_tp(i, _):
        p = lax.rem(mt + 1 + i, TP)
        pl.semaphore_signal(barrier, inc=1, device_id={"tp": p}, device_id_type=MESH)
        return 0

    lax.fori_loop(0, TP - 1, greet_tp, 0)
    call[me] = counts[...]
    rrecv[me] = rsend[me]
    pl.semaphore_wait(barrier, N - 1 + TP - 1)

    def send_counts(i, _):
        seq_copy(counts, call.at[me], s_c, r_c, partner(i)).start()
        return 0

    lax.fori_loop(0, N - 1, send_counts, 0)

    def send_part(i, _):
        p = partner(i)
        seq_copy(rsend.at[p], rrecv.at[me], s_p, r_p, p).start()
        return 0

    lax.fori_loop(0, N - 1, send_part, 0)

    many = call.at[pl.ds(0, N - 1)]
    seq_copy(many, many, s_c, r_c, lax.rem(me + 1, N)).wait_recv()
    earlier = lax.broadcasted_iota(I32, (N, 1, BLOCK), 0) < me
    offset = jnp.sum(jnp.sum(jnp.where(earlier, call[...], 0), axis=0))
    turn = (0 - offset) & (N - 1)
    send[...] = twice[pl.ds(turn, N)]
    xsend[...] = xtwice[pl.ds(turn, N)]
    recv[me] = send[me]
    xrecv[me] = xsend[me]

    def send_slab(i, _):
        p = partner(i)
        seq_copy(send.at[p], recv.at[me], s_m, r_m, p).start()
        seq_copy(xsend.at[p], xrecv.at[me], s_x, r_x, p).start()
        return 0

    lax.fori_loop(0, FIRST, send_slab, 0)

    many_p = rrecv.at[pl.ds(0, N - 1)]
    seq_copy(many_p, many_p, s_p, r_p, lax.rem(me + 1, N)).wait_recv()
    own = own_ref[:, HD : HD + 128]
    peaks = rrecv[:, :, HD : HD + 128]
    peak = jnp.maximum(jnp.max(peaks, axis=0), own)
    w = jnp.exp(peaks - peak[None])
    own_p = jnp.exp(own - peak)
    tot = jnp.sum(w * rrecv[:, :, HD + 128 : HD + 256], axis=0) + own_p
    for c in range(2):
        lanes = slice(128 * c, 128 * (c + 1))
        wsum = jnp.sum(w * rrecv[:, :, lanes], axis=0) + own_p * own_ref[:, lanes]
        gsend[:, lanes] = (wsum / tot).astype(BF16).astype(F32)
    grecv[me] = gsend[...]

    def send_row(i, _):
        seq_copy(gsend, grecv.at[me], s_g, r_g, partner(i)).start()
        return 0

    lax.fori_loop(0, N - 1, send_row, 0)
    lax.fori_loop(FIRST, SECOND, send_slab, 0)

    many_g = grecv.at[pl.ds(0, N - 1)]
    seq_copy(many_g, many_g, s_g, r_g, lax.rem(me + 1, N)).wait_recv()
    rows = grecv[...].reshape(N, HD).astype(BF16)
    tsend[...] = jnp.dot(rows, ow_ref[...], preferred_element_type=F32).reshape(TP, 8, 128)
    trecv[mt] = tsend[mt]

    def send_tp(i, _):
        p = lax.rem(mt + 1 + i, TP)
        tp_copy(tsend.at[p], trecv.at[mt], p).start()
        return 0

    lax.fori_loop(0, TP - 1, send_tp, 0)
    lax.fori_loop(SECOND, N - 1, send_slab, 0)

    many_t = trecv.at[pl.ds(0, TP - 1)]
    tp_copy(many_t, many_t, lax.rem(mt + 1, TP)).wait_recv()
    lo_ref[...] = jnp.sum(trecv[...], axis=0)[0:6, 0:32].astype(BF16)

    for buf, s_sem, r_sem in ((recv, s_m, r_m), (xrecv, s_x, r_x)):
        many = buf.at[pl.ds(0, N - 1)]
        seq_copy(many, many, s_sem, r_sem, lax.rem(me + 1, N)).wait_recv()
    for buf, s_sem, r_sem in (
        (call, s_c, r_c), (rrecv, s_p, r_p), (grecv, s_g, r_g), (recv, s_m, r_m), (xrecv, s_x, r_x)
    ):
        many = buf.at[pl.ds(0, N - 1)]
        seq_copy(many, many, s_sem, r_sem, lax.rem(me + 1, N)).wait_send()
    tp_copy(many_t, many_t, lax.rem(mt + 1, TP)).wait_send()


def exchange(counts, rsend, twice, xtwice, own, ow):
    vmem = pl.BlockSpec(memory_space=pltpu.VMEM)
    outs = [((N, 1, BLOCK), I32), ((N, SLAB, 2 * HD), BF16), ((N, 2, HD), BF16), ((6, 32), BF16)]
    scratch = [
        ((N, SLAB, 2 * HD), BF16),
        ((N, 2, HD), BF16),
        ((N, 1, 2 * HD), F32),
        ((1, HD), F32),
        ((N, 1, HD), F32),
        ((TP, 8, 128), F32),
        ((TP, 8, 128), F32),
    ]
    return pl.pallas_call(
        swap_kernel,
        name="swap",
        out_shape=tuple(jax.ShapeDtypeStruct(s, d) for s, d in outs),
        in_specs=[vmem] * 6,
        out_specs=(vmem,) * len(outs),
        scratch_shapes=[pltpu.VMEM(s, d) for s, d in scratch] + [pltpu.SemaphoreType.DMA] * 12,
        compiler_params=pltpu.CompilerParams(
            collective_id=0, has_side_effects=True, vmem_limit_bytes=40 << 20
        ),
    )(counts, rsend, twice, xtwice, own, ow)


def local(body, name, outs, scratch, *args):
    vmem = pl.BlockSpec(memory_space=pltpu.VMEM)
    return pl.pallas_call(
        body,
        name=name,
        out_shape=tuple(jax.ShapeDtypeStruct(s, d) for s, d in outs),
        in_specs=[vmem] * len(args),
        out_specs=(vmem,) * len(outs),
        scratch_shapes=[pltpu.VMEM(s, d) for s, d in scratch],
        compiler_params=pltpu.CompilerParams(vmem_limit_bytes=40 << 20),
    )(*args)


def on_device(ck, cv, keep, w, req, q, nk, nv, ow):
    keep2 = keep.reshape(NB, BLOCK)
    w2 = w.reshape(NB, BLOCK)
    req2 = jnp.pad(req, (0, BLOCK - REQS)).reshape(1, BLOCK)
    ow2 = jnp.pad(ow, ((0, 0), (0, 128 - ow.shape[1])))
    twice, xtwice, counts, rsend, own = local(
        pack_kernel, "pack",
        [
            ((2 * N, SLAB, 2 * HD), BF16), ((2 * N, 2, HD), BF16), ((1, BLOCK), I32),
            ((N, 1, 2 * HD), F32), ((1, HD + 128), F32),
        ],
        [((K_DEV, 2 * HD), BF16), ((N, 2 * HD), F32), ((K_DEV - MAIN, 2 * HD), F32)],
        ck, cv, keep2, w2, req2, q, nk, nv,
    )
    counts, recv, xrecv, lo = exchange(counts, rsend, twice, xtwice, own, ow2)
    pk, pv, pb, pr = local(
        place_kernel, "place",
        [((K_DEV, HD), BF16), ((K_DEV, HD), BF16), ((1, K_DEV), BF16), ((1, K_DEV), I32)],
        [((N, BLOCK), I32), ((BLOCK, 2 * HD), F32), ((1, MAIN), I32)],
        counts, recv, xrecv, req2,
    )
    return pk, pv, pb.reshape(K_DEV), pr.reshape(K_DEV), lo


def solution(mesh):
    in_specs = (
        P("seq", "tp"), P("seq", "tp"), P("seq"), P("seq"), P(),
        P(None, "tp"), P(None, "tp"), P(None, "tp"), P("tp", "seq"),
    )
    out_specs = (P("seq", "tp"), P("seq", "tp"), P("seq"), P("seq"), P("tp", "seq"))
    return jax.shard_map(on_device, mesh=mesh, in_specs=in_specs, out_specs=out_specs, check_vma=False)
```

```python
import jax
import jax.numpy as jnp
from jax import lax
from jax.experimental import pallas as pl
from jax.experimental.pallas import tpu as pltpu
from jax.sharding import PartitionSpec as P

MESH = pl.DeviceIdType.MESH
F32, BF16, I32 = jnp.float32, jnp.bfloat16, jnp.int32

N = 64
TP = 8
HD = 256
BLOCK = 128
NB = 16
ROWS = 2048
REQS = 48
K_DEV = 1040
SLAB = 16
MAIN = N * SLAB
TILE = 208
TILES = K_DEV // TILE
NEG = -1e30
NX = 4
NZ = N // NX
CUTS = (0, 12, 24, 36, 48, N - 1)


def iota(shape, dim):
    return lax.broadcasted_iota(I32, shape, dim)


def entry_of(t):
    return jnp.where(t < MAIN, (t & (SLAB - 1)) * N + (t >> 4), t)


def pack_kernel(
    k_ref, v_ref, keep_ref, w_ref, req_ref, q_ref, nk_ref, nv_ref,
    twice, xtwice, counts, rsend, own_ref, grp, part, xf
):
    me = lax.axis_index("seq")
    keep = keep_ref[...]
    keepf = keep.astype(F32)
    upper = (iota((BLOCK, BLOCK), 0) < iota((BLOCK, BLOCK), 1)).astype(BF16)
    within = jnp.dot(keepf.astype(BF16), upper, preferred_element_type=F32)
    kept_col = jnp.sum(keepf, axis=1, keepdims=True)
    size_col = kept_col + 1.0
    eye = iota((NB, BLOCK), 0) == iota((NB, BLOCK), 1)
    size_row = jnp.sum(jnp.where(eye, size_col, 0.0), axis=0, keepdims=True)
    base_col = jnp.sum(
        jnp.where(iota((NB, BLOCK), 1) < iota((NB, BLOCK), 0), size_row, 0.0), axis=1, keepdims=True
    )
    fold_col = base_col + kept_col
    counts[...] = size_row.astype(I32)
    entry = jnp.where(keep == 1, base_col + within, fold_col).astype(I32)
    tgt_in = jnp.where(entry < MAIN, ((entry & (N - 1)) << 4) | (entry >> 6), entry)
    dropped = w_ref[...] * (1 - keep)
    val_in = jnp.where(keep == 1, 1, dropped).astype(F32)
    denom_col = jnp.sum(dropped.astype(F32), axis=1, keepdims=True)
    inv_row = jnp.sum(jnp.where(eye, 1.0 / denom_col, 0.0), axis=0, keepdims=True)
    fold_row = jnp.sum(jnp.where(eye, fold_col, 0.0), axis=0, keepdims=True).astype(I32)
    fold_row = jnp.where(iota((1, BLOCK), 1) < NB, fold_row, -1)

    def group(j, _):
        start = pl.multiple_of(j * TILE, 16)
        t = iota((TILE, BLOCK), 0) + start
        pieces = [
            jnp.where(t == tgt_in[b : b + 1, :], val_in[b : b + 1, :], 0.0).astype(BF16)
            for b in range(NB)
        ]
        sel = jnp.concatenate(pieces, axis=1)
        is_fold = entry_of(t) == fold_row
        scale = jnp.sum(jnp.where(is_fold, inv_row, 0.0), axis=1, keepdims=True)
        scale = jnp.where(scale > 0.0, scale, 1.0)
        kk = jnp.dot(sel, k_ref[...], preferred_element_type=F32)
        vv = jnp.dot(sel, v_ref[...], preferred_element_type=F32)
        grp[pl.ds(start, TILE), 0:HD] = (kk * scale).astype(BF16)
        grp[pl.ds(start, TILE), HD : 2 * HD] = (vv * scale).astype(BF16)
        return 0

    lax.fori_loop(0, TILES, group, 0)
    slabs = grp[0:MAIN, :].reshape(N, SLAB, 2 * HD)
    twice[0:N] = slabs
    twice[N : 2 * N] = slabs
    xf[...] = grp[MAIN:K_DEV, :].astype(F32)
    xtwice[...] = jnp.zeros(xtwice.shape, BF16)
    for c in range(K_DEV - MAIN):
        row = xf[c : c + 1, :]
        pair = jnp.concatenate([row[:, 0:HD], row[:, HD : 2 * HD]], axis=0).astype(BF16)
        xtwice[c] = pair
        xtwice[N + c] = pair

    spread = spread_rows()
    q64 = jnp.dot(spread, q_ref[...], preferred_element_type=F32)
    srow = iota((N, BLOCK), 0)
    lane = iota((N, BLOCK), 1)
    used = (srow & 7) < 6
    starts, ends = request_blocks(req_ref)
    gblock = (lane + me * NB).astype(F32)
    low = jnp.sum(jnp.where(gblock < starts, size_row, 0.0), axis=1, keepdims=True)
    high = jnp.sum(jnp.where((gblock < ends) & used, size_row, 0.0), axis=1, keepdims=True)
    log_col = jnp.log(float(BLOCK) - kept_col).astype(BF16).astype(F32)
    e_row = entry_of(iota((1, K_DEV), 1)).astype(F32)
    bias_row = jnp.sum(
        jnp.where(jnp.broadcast_to(e_row, (NB, K_DEV)) == fold_col, log_col, 0.0), axis=0, keepdims=True
    )
    scores = lax.dot_general(
        q64.astype(BF16), grp[:, 0:HD], (((1,), (1,)), ((), ())), preferred_element_type=F32
    )
    scores = scores * (1.0 / 16.0) + bias_row
    member = (e_row >= low) & (e_row < high)
    scores = jnp.where(member, scores, NEG)
    peak = jnp.max(scores, axis=1, keepdims=True)
    probs = jnp.where(member, jnp.exp(scores - peak), 0.0)
    total = jnp.sum(probs, axis=1, keepdims=True)
    part[:, 0:HD] = jnp.dot(probs.astype(BF16), grp[:, HD : 2 * HD], preferred_element_type=F32)
    part[:, HD : HD + 128] = jnp.broadcast_to(peak, (N, 128))
    part[:, HD + 128 : HD + 256] = jnp.broadcast_to(total, (N, 128))

    def fill_part(s, _):
        for x in range(NX):
            rsend[x, s] = part[pl.ds(x * NZ + s, 1), :]
        return 0

    lax.fori_loop(0, NZ, fill_part, 0)

    row = (me & (NX - 1)) * NZ + (me >> 2)
    mine = ((6 * (row >> 3) + (row & 7) == iota((8, REQS), 1)) & ((row & 7) < 6)).astype(BF16)
    qr = jnp.dot(mine, q_ref[...], preferred_element_type=F32)
    kr = jnp.dot(mine, nk_ref[...], preferred_element_type=F32)
    nv = jnp.dot(mine, nv_ref[...], preferred_element_type=F32)[0:1, :]
    own = jnp.sum(qr * kr, axis=1, keepdims=True)[0:1, :] * (1.0 / 16.0)
    own_ref[:, 0:HD] = nv
    own_ref[:, HD : HD + 128] = jnp.broadcast_to(own, (1, 128))


def spread_rows():
    row, req = iota((N, REQS), 0), iota((N, REQS), 1)
    return ((6 * (row >> 3) + (row & 7) == req) & ((row & 7) < 6)).astype(BF16)


def request_blocks(req_ref):
    srow = iota((N, REQS), 0)
    lane = iota((N, REQS), 1)
    rid = 6 * (srow >> 3) + (srow & 7)
    req_row = req_ref[...].astype(F32)
    ends = jnp.sum(jnp.where(lane <= rid, req_row, 0.0), axis=1, keepdims=True)
    starts = jnp.sum(jnp.where(lane < rid, req_row, 0.0), axis=1, keepdims=True)
    return starts, ends


def slot_tables(call, req_ref, me, pb_ref, pr_ref, tgt, xtgt):
    srow = iota((N, BLOCK), 0)
    lane = iota((N, BLOCK), 1)
    _, ends = request_blocks(req_ref)
    sizes = call[...].reshape(N, BLOCK).astype(F32)
    sizes16 = sizes.astype(BF16)
    n_col = jnp.sum(sizes, axis=1, keepdims=True)
    before64 = (iota((N, N), 1) < iota((N, N), 0)).astype(BF16)
    off_col = jnp.sum(jnp.dot(before64, sizes16, preferred_element_type=F32), axis=1, keepdims=True)
    upto = (iota((BLOCK, BLOCK), 0) <= iota((BLOCK, BLOCK), 1)).astype(BF16)
    block_end = off_col + jnp.dot(sizes16, upto, preferred_element_type=F32)
    drops = jnp.where(lane < NB, float(BLOCK + 1) - sizes, 1.0)
    logs = jnp.log(drops).astype(BF16).astype(F32)
    j_row = (iota((1, K_DEV), 1) * N + me).astype(F32)
    bias_out = jnp.zeros((N, K_DEV), F32)
    for b in range(NB):
        hit = (block_end[:, b : b + 1] - 1.0) == j_row
        bias_out = jnp.where(hit, logs[:, b : b + 1], bias_out)
    pb_ref[...] = jnp.sum(bias_out, axis=0, keepdims=True).astype(BF16)
    last = ends.astype(I32) - 1
    pick = (iota((N, N), 1) == (last >> 4)).astype(F32)
    picked = jnp.dot(pick, block_end, preferred_element_type=F32, precision=lax.Precision.HIGHEST)
    req_end = jnp.sum(jnp.where(lane == (last & 15), picked, 0.0), axis=1, keepdims=True)
    past = ((req_end <= j_row) & ((iota((N, K_DEV), 0) & 7) < 6)).astype(F32)
    owner = jnp.sum(past, axis=0, keepdims=True)
    every = jnp.sum(n_col, axis=0, keepdims=True)
    pr_ref[...] = jnp.where(j_row < every, owner, -1.0).astype(I32)

    off_i = off_col.astype(I32)
    c_col = (me - off_i) & (N - 1)
    k0_col = ((off_i + c_col) >> 6).astype(F32)
    lim_col = n_col - c_col.astype(F32)
    col = iota((N, MAIN), 1)
    is_src = iota((N, MAIN), 0) == (col >> 4)
    k0 = jnp.sum(jnp.where(is_src, k0_col, 0.0), axis=0, keepdims=True)
    lim = jnp.sum(jnp.where(is_src, lim_col, 0.0), axis=0, keepdims=True)
    q = (col[0:1, :] & (SLAB - 1)).astype(F32)
    tgt[...] = jnp.where(q * N < lim, k0 + q, -1.0).astype(I32)
    is_src = srow == lane
    k0 = jnp.sum(jnp.where(is_src, k0_col, 0.0), axis=0, keepdims=True)
    lim = jnp.sum(jnp.where(is_src, lim_col, 0.0), axis=0, keepdims=True)
    xtgt[...] = jnp.where(lim > float(MAIN), k0 + float(SLAB), -1.0).astype(I32)


def place_kernel(recv, xrecv, tgt, xtgt, pk_ref, pv_ref, x2):
    x2[...] = jnp.zeros(x2.shape, F32)

    def fill_extra(i, _):
        pair = xrecv[i].astype(F32)
        x2[pl.ds(i, 1), 0:HD] = pair[0:1, :]
        x2[pl.ds(i, 1), HD : 2 * HD] = pair[1:2, :]
        return 0

    lax.fori_loop(0, N, fill_extra, 0, unroll=8)

    def place(j, _):
        start = pl.multiple_of(j * TILE, 16)
        sel = jnp.where(iota((TILE, MAIN), 0) + start == tgt[...], 1.0, 0.0).astype(BF16)
        xsel = jnp.where(iota((TILE, BLOCK), 0) + start == xtgt[...], 1.0, 0.0).astype(BF16)
        rows = recv[...].reshape(MAIN, 2 * HD)
        got = jnp.dot(sel, rows, preferred_element_type=F32)
        got = got + jnp.dot(xsel, x2[...].astype(BF16), preferred_element_type=F32)
        pk_ref[pl.ds(start, TILE), :] = got[:, 0:HD].astype(BF16)
        pv_ref[pl.ds(start, TILE), :] = got[:, HD : 2 * HD].astype(BF16)
        return 0

    lax.fori_loop(0, TILES, place, 0)


def step_of(i):
    half = (i + 1) // 2
    return N // 2 + half * (1 - 2 * (i % 2))


def swap_kernel(
    counts, rsend, twice, xtwice, own_ref, ow_ref, req_ref,
    recv, xrecv, lo_ref, pb_ref, pr_ref, tgt, xtgt,
    call, send, xsend, prow, zsend, pcol, gsend, grecv, tsend, trecv,
    s_c, r_c, s_p, r_p, s_q, r_q, s_m, r_m, s_x, r_x, s_g, r_g, s_h, r_h, s_t, r_t,
):
    me = lax.axis_index("seq")
    mt = lax.axis_index("tp")
    z, x = lax.div(me, NX), lax.rem(me, NX)

    def seq_copy(src, dst, s_sem, r_sem, p):
        return pltpu.make_async_remote_copy(
            src, dst, s_sem, r_sem, device_id={"seq": p}, device_id_type=MESH
        )

    def tp_copy(src, dst, p):
        return pltpu.make_async_remote_copy(
            src, dst, s_t, r_t, device_id={"tp": p}, device_id_type=MESH
        )

    def partner(i):
        return lax.rem(me + step_of(i), N)

    def z_part(i):
        return lax.rem(z + 1 + i, NZ)

    def x_part(i):
        return lax.rem(x + 1 + i, NX)

    near = lax.rem(me + 1, N)
    barrier = pltpu.get_barrier_semaphore()

    def greet(i, _):
        pl.semaphore_signal(barrier, inc=1, device_id={"seq": partner(i)}, device_id_type=MESH)
        return 0

    lax.fori_loop(0, N - 1, greet, 0)

    def greet_tp(i, _):
        p = lax.rem(mt + 1 + i, TP)
        pl.semaphore_signal(barrier, inc=1, device_id={"tp": p}, device_id_type=MESH)
        return 0

    lax.fori_loop(0, TP - 1, greet_tp, 0)
    call[me] = counts[...]
    prow[x] = rsend[x]
    pl.semaphore_wait(barrier, N - 1 + TP - 1)

    def send_counts(i, _):
        seq_copy(counts, call.at[me], s_c, r_c, partner(i)).start()
        return 0

    lax.fori_loop(0, N - 1, send_counts, 0)

    def send_part(i, _):
        p = x_part(i)
        seq_copy(rsend.at[p], prow.at[x], s_p, r_p, z * NX + p).start()
        return 0

    lax.fori_loop(0, NX - 1, send_part, 0)

    all_c = call.at[pl.ds(0, N - 1)]
    seq_copy(all_c, all_c, s_c, r_c, near).wait_recv()
    earlier = lax.broadcasted_iota(I32, (N, 1, BLOCK), 0) < me
    offset = jnp.sum(jnp.sum(jnp.where(earlier, call[...], 0), axis=0))
    turn = (0 - offset) & (N - 1)
    send[...] = twice[pl.ds(turn, N)]
    xsend[...] = xtwice[pl.ds(turn, N)]

    def send_slab(i, _):
        p = partner(i)
        seq_copy(send.at[p], recv.at[me], s_m, r_m, p).start()
        seq_copy(xsend.at[p], xrecv.at[me], s_x, r_x, p).start()
        return 0

    lax.fori_loop(CUTS[0], CUTS[1], send_slab, 0)
    recv[me] = send[me]
    xrecv[me] = xsend[me]

    all_p = prow.at[pl.ds(0, NX - 1)]
    seq_copy(all_p, all_p, s_p, r_p, near).wait_recv()
    peaks = prow[:, :, :, HD : HD + 128]
    peak = jnp.max(peaks, axis=0)
    w = jnp.exp(peaks - peak[None])
    for c in (0, 1, 3):
        lanes = slice(128 * c, 128 * (c + 1))
        zsend[:, :, lanes] = jnp.sum(w * prow[:, :, :, lanes], axis=0)
    zsend[:, :, HD : HD + 128] = peak
    pcol[z] = zsend[z]

    def send_merged(i, _):
        p = z_part(i)
        seq_copy(zsend.at[p], pcol.at[z], s_q, r_q, p * NX + x).start()
        return 0

    lax.fori_loop(0, NZ - 1, send_merged, 0)
    lax.fori_loop(CUTS[1], CUTS[2], send_slab, 0)

    all_q = pcol.at[pl.ds(0, NZ - 1)]
    seq_copy(all_q, all_q, s_q, r_q, near).wait_recv()
    own = own_ref[:, HD : HD + 128]
    peaks = pcol[:, :, HD : HD + 128]
    peak = jnp.maximum(jnp.max(peaks, axis=0), own)
    w = jnp.exp(peaks - peak[None])
    own_p = jnp.exp(own - peak)
    tot = jnp.sum(w * pcol[:, :, HD + 128 : HD + 256], axis=0) + own_p
    for c in range(2):
        lanes = slice(128 * c, 128 * (c + 1))
        wsum = jnp.sum(w * pcol[:, :, lanes], axis=0) + own_p * own_ref[:, lanes]
        gsend[:, lanes] = (wsum / tot).astype(BF16).astype(F32)
    grecv[x, z] = gsend[...]

    def send_row(i, _):
        seq_copy(gsend, grecv.at[x, z], s_g, r_g, z_part(i) * NX + x).start()
        return 0

    lax.fori_loop(0, NZ - 1, send_row, 0)
    lax.fori_loop(CUTS[2], CUTS[3], send_slab, 0)

    all_g = grecv.at[0, pl.ds(0, NZ - 1)]
    seq_copy(all_g, all_g, s_g, r_g, near).wait_recv()

    def send_rows(i, _):
        seq_copy(grecv.at[x], grecv.at[x], s_h, r_h, z * NX + x_part(i)).start()
        return 0

    lax.fori_loop(0, NX - 1, send_rows, 0)
    lax.fori_loop(CUTS[3], CUTS[4], send_slab, 0)

    all_h = grecv.at[pl.ds(0, NX - 1)]
    seq_copy(all_h, all_h, s_h, r_h, near).wait_recv()
    rows = grecv[...].reshape(N, HD).astype(BF16)
    wide = lax.dot_general(rows, ow_ref[...], (((1,), (1,)), ((), ())), preferred_element_type=F32)
    wide = jnp.concatenate([wide, jnp.zeros((N, 96), F32)], axis=1)
    tsend[...] = wide.reshape(TP, 8, 128)
    trecv[mt] = tsend[mt]

    def send_tp(i, _):
        p = lax.rem(mt + 1 + i, TP)
        tp_copy(tsend.at[p], trecv.at[mt], p).start()
        return 0

    lax.fori_loop(0, TP - 1, send_tp, 0)
    lax.fori_loop(CUTS[4], CUTS[5], send_slab, 0)
    slot_tables(call, req_ref, me, pb_ref, pr_ref, tgt, xtgt)

    all_t = trecv.at[pl.ds(0, TP - 1)]
    tp_copy(all_t, all_t, lax.rem(mt + 1, TP)).wait_recv()
    lo_ref[...] = jnp.sum(trecv[...], axis=0)[0:6, 0:32].astype(BF16)

    all_m = recv.at[pl.ds(0, N - 1)]
    all_x = xrecv.at[pl.ds(0, N - 1)]
    for part, s_sem, r_sem in ((all_m, s_m, r_m), (all_x, s_x, r_x)):
        seq_copy(part, part, s_sem, r_sem, near).wait_recv()
    for part, s_sem, r_sem in (
        (all_c, s_c, r_c), (all_p, s_p, r_p), (all_q, s_q, r_q), (all_g, s_g, r_g),
        (all_h, s_h, r_h), (all_m, s_m, r_m), (all_x, s_x, r_x),
    ):
        seq_copy(part, part, s_sem, r_sem, near).wait_send()
    tp_copy(all_t, all_t, lax.rem(mt + 1, TP)).wait_send()


def exchange(counts, rsend, twice, xtwice, own, ow, req):
    vmem = pl.BlockSpec(memory_space=pltpu.VMEM)
    outs = [
        ((N, SLAB, 2 * HD), BF16), ((N, 2, HD), BF16), ((6, 32), BF16),
        ((1, K_DEV), BF16), ((1, K_DEV), I32), ((1, MAIN), I32), ((1, BLOCK), I32),
    ]
    scratch = [
        ((N, 1, BLOCK), I32),
        ((N, SLAB, 2 * HD), BF16),
        ((N, 2, HD), BF16),
        ((NX, NZ, 1, 2 * HD), F32),
        ((NZ, 1, 2 * HD), F32),
        ((NZ, 1, 2 * HD), F32),
        ((1, HD), F32),
        ((NX, NZ, 1, HD), F32),
        ((TP, 8, 128), F32),
        ((TP, 8, 128), F32),
    ]
    return pl.pallas_call(
        swap_kernel,
        name="swap",
        out_shape=tuple(jax.ShapeDtypeStruct(s, d) for s, d in outs),
        in_specs=[vmem] * 7,
        out_specs=(vmem,) * len(outs),
        scratch_shapes=[pltpu.VMEM(s, d) for s, d in scratch] + [pltpu.SemaphoreType.DMA] * 16,
        compiler_params=pltpu.CompilerParams(
            collective_id=0, has_side_effects=True, vmem_limit_bytes=40 << 20
        ),
    )(counts, rsend, twice, xtwice, own, ow, req)


def local(body, name, outs, scratch, *args, fetch=False):
    vmem = pl.BlockSpec(memory_space=pltpu.VMEM)
    whole = {"in_specs": [vmem] * len(args)}
    if fetch:
        whole = {
            "grid": (1,),
            "in_specs": [pl.BlockSpec(a.shape, lambda i: (0, 0)) for a in args],
        }
    return pl.pallas_call(
        body,
        name=name,
        out_shape=tuple(jax.ShapeDtypeStruct(s, d) for s, d in outs),
        out_specs=(vmem,) * len(outs),
        scratch_shapes=[pltpu.VMEM(s, d) for s, d in scratch],
        compiler_params=pltpu.CompilerParams(vmem_limit_bytes=40 << 20),
        **whole,
    )(*args)


def on_device(ck, cv, keep, w, req, q, nk, nv, ow):
    keep2 = keep.reshape(NB, BLOCK)
    w2 = w.reshape(NB, BLOCK)
    req2 = req.reshape(1, REQS)
    twice, xtwice, counts, rsend, own = local(
        pack_kernel, "pack",
        [
            ((2 * N, SLAB, 2 * HD), BF16), ((2 * N, 2, HD), BF16), ((1, BLOCK), I32),
            ((NX, NZ, 1, 2 * HD), F32), ((1, HD + 128), F32),
        ],
        [((K_DEV, 2 * HD), BF16), ((N, 2 * HD), F32), ((K_DEV - MAIN, 2 * HD), F32)],
        ck, cv, keep2, w2, req2, q, nk, nv,
        fetch=True,
    )
    recv, xrecv, lo, pb, pr, tgt, xtgt = exchange(counts, rsend, twice, xtwice, own, ow.T, req2)
    pk, pv = local(
        place_kernel, "place",
        [((K_DEV, HD), BF16), ((K_DEV, HD), BF16)], [((BLOCK, 2 * HD), F32)],
        recv, xrecv, tgt, xtgt,
    )
    return pk, pv, pb.reshape(K_DEV), pr.reshape(K_DEV), lo


def solution(mesh):
    in_specs = (
        P("seq", "tp"), P("seq", "tp"), P("seq"), P("seq"), P(),
        P(None, "tp"), P(None, "tp"), P(None, "tp"), P("tp", "seq"),
    )
    out_specs = (P("seq", "tp"), P("seq", "tp"), P("seq"), P("seq"), P("tp", "seq"))
    return jax.shard_map(on_device, mesh=mesh, in_specs=in_specs, out_specs=out_specs, check_vma=False)
```

```python
import jax
import jax.numpy as jnp
from jax import lax
from jax.experimental import pallas as pl
from jax.experimental.pallas import tpu as pltpu
from jax.sharding import PartitionSpec as P

MESH = pl.DeviceIdType.MESH
F32, BF16, I32 = jnp.float32, jnp.bfloat16, jnp.int32

N = 64
TP = 8
HD = 256
BLOCK = 128
NB = 16
ROWS = 2048
REQS = 48
K_DEV = 1040
SLAB = 16
MAIN = N * SLAB
TILE = 208
TILES = K_DEV // TILE
NEG = -1e30
NX = 4
NZ = N // NX
CUTS = (0, 12, 24, 36, 48, N - 1)


def iota(shape, dim):
    return lax.broadcasted_iota(I32, shape, dim)


def entry_of(t):
    return jnp.where(t < MAIN, (t & (SLAB - 1)) * N + (t >> 4), t)


def pack_kernel(
    k_ref, v_ref, keep_ref, w_ref, req_ref, q_ref, nk_ref, nv_ref,
    twice, xtwice, counts, rsend, own_ref, grp, part, xf
):
    me = lax.axis_index("seq")
    keep = keep_ref[...]
    keepf = keep.astype(F32)
    upper = (iota((BLOCK, BLOCK), 0) < iota((BLOCK, BLOCK), 1)).astype(BF16)
    within = jnp.dot(keepf.astype(BF16), upper, preferred_element_type=F32)
    kept_col = jnp.sum(keepf, axis=1, keepdims=True)
    size_col = kept_col + 1.0
    eye = iota((NB, BLOCK), 0) == iota((NB, BLOCK), 1)
    size_row = jnp.sum(jnp.where(eye, size_col, 0.0), axis=0, keepdims=True)
    base_col = jnp.sum(
        jnp.where(iota((NB, BLOCK), 1) < iota((NB, BLOCK), 0), size_row, 0.0), axis=1, keepdims=True
    )
    fold_col = base_col + kept_col
    counts[...] = size_row.astype(I32)
    entry = jnp.where(keep == 1, base_col + within, fold_col).astype(I32)
    tgt_in = jnp.where(entry < MAIN, ((entry & (N - 1)) << 4) | (entry >> 6), entry)
    dropped = w_ref[...] * (1 - keep)
    val_in = jnp.where(keep == 1, 1, dropped).astype(F32)
    denom_col = jnp.sum(dropped.astype(F32), axis=1, keepdims=True)
    inv_row = jnp.sum(jnp.where(eye, 1.0 / denom_col, 0.0), axis=0, keepdims=True)
    fold_row = jnp.sum(jnp.where(eye, fold_col, 0.0), axis=0, keepdims=True).astype(I32)
    fold_row = jnp.where(iota((1, BLOCK), 1) < NB, fold_row, -1)

    def group(j, _):
        start = pl.multiple_of(j * TILE, 16)
        t = iota((TILE, BLOCK), 0) + start
        pieces = [
            jnp.where(t == tgt_in[b : b + 1, :], val_in[b : b + 1, :], 0.0).astype(BF16)
            for b in range(NB)
        ]
        sel = jnp.concatenate(pieces, axis=1)
        is_fold = entry_of(t) == fold_row
        scale = jnp.sum(jnp.where(is_fold, inv_row, 0.0), axis=1, keepdims=True)
        scale = jnp.where(scale > 0.0, scale, 1.0)
        kk = jnp.dot(sel, k_ref[...], preferred_element_type=F32)
        vv = jnp.dot(sel, v_ref[...], preferred_element_type=F32)
        grp[pl.ds(start, TILE), 0:HD] = (kk * scale).astype(BF16)
        grp[pl.ds(start, TILE), HD : 2 * HD] = (vv * scale).astype(BF16)
        return 0

    lax.fori_loop(0, TILES, group, 0)
    slabs = grp[0:MAIN, :].reshape(N, SLAB, 2 * HD)
    twice[0:N] = slabs
    twice[N : 2 * N] = slabs
    xf[...] = grp[MAIN:K_DEV, :].astype(F32)
    xtwice[...] = jnp.zeros(xtwice.shape, BF16)
    for c in range(K_DEV - MAIN):
        row = xf[c : c + 1, :]
        pair = jnp.concatenate([row[:, 0:HD], row[:, HD : 2 * HD]], axis=0).astype(BF16)
        xtwice[c] = pair
        xtwice[N + c] = pair

    spread = spread_rows()
    q64 = jnp.dot(spread, q_ref[...], preferred_element_type=F32)
    srow = iota((N, BLOCK), 0)
    lane = iota((N, BLOCK), 1)
    used = (srow & 7) < 6
    starts, ends = request_blocks(req_ref)
    gblock = (lane + me * NB).astype(F32)
    low = jnp.sum(jnp.where(gblock < starts, size_row, 0.0), axis=1, keepdims=True)
    high = jnp.sum(jnp.where((gblock < ends) & used, size_row, 0.0), axis=1, keepdims=True)
    log_col = jnp.log(float(BLOCK) - kept_col).astype(BF16).astype(F32)
    e_row = entry_of(iota((1, K_DEV), 1)).astype(F32)
    bias_row = jnp.sum(
        jnp.where(jnp.broadcast_to(e_row, (NB, K_DEV)) == fold_col, log_col, 0.0), axis=0, keepdims=True
    )
    scores = lax.dot_general(
        q64.astype(BF16), grp[:, 0:HD], (((1,), (1,)), ((), ())), preferred_element_type=F32
    )
    scores = scores * (1.0 / 16.0) + bias_row
    member = (e_row >= low) & (e_row < high)
    scores = jnp.where(member, scores, NEG)
    peak = jnp.max(scores, axis=1, keepdims=True)
    probs = jnp.where(member, jnp.exp(scores - peak), 0.0)
    total = jnp.sum(probs, axis=1, keepdims=True)
    part[:, 0:HD] = jnp.dot(probs.astype(BF16), grp[:, HD : 2 * HD], preferred_element_type=F32)
    part[:, HD : HD + 128] = jnp.broadcast_to(peak, (N, 128))
    part[:, HD + 128 : HD + 256] = jnp.broadcast_to(total, (N, 128))

    def fill_part(s, _):
        for x in range(NX):
            rsend[x, s] = part[pl.ds(x * NZ + s, 1), :]
        return 0

    lax.fori_loop(0, NZ, fill_part, 0)

    row = (me & (NX - 1)) * NZ + (me >> 2)
    mine = ((6 * (row >> 3) + (row & 7) == iota((8, REQS), 1)) & ((row & 7) < 6)).astype(BF16)
    qr = jnp.dot(mine, q_ref[...], preferred_element_type=F32)
    kr = jnp.dot(mine, nk_ref[...], preferred_element_type=F32)
    nv = jnp.dot(mine, nv_ref[...], preferred_element_type=F32)[0:1, :]
    own = jnp.sum(qr * kr, axis=1, keepdims=True)[0:1, :] * (1.0 / 16.0)
    own_ref[:, 0:HD] = nv
    own_ref[:, HD : HD + 128] = jnp.broadcast_to(own, (1, 128))


def spread_rows():
    row, req = iota((N, REQS), 0), iota((N, REQS), 1)
    return ((6 * (row >> 3) + (row & 7) == req) & ((row & 7) < 6)).astype(BF16)


def request_blocks(req_ref):
    srow = iota((N, REQS), 0)
    lane = iota((N, REQS), 1)
    rid = 6 * (srow >> 3) + (srow & 7)
    req_row = req_ref[...].astype(F32)
    ends = jnp.sum(jnp.where(lane <= rid, req_row, 0.0), axis=1, keepdims=True)
    starts = jnp.sum(jnp.where(lane < rid, req_row, 0.0), axis=1, keepdims=True)
    return starts, ends


def slot_tables(call, req_ref, me, pb_ref, pr_ref, tgt, xtgt):
    srow = iota((N, BLOCK), 0)
    lane = iota((N, BLOCK), 1)
    _, ends = request_blocks(req_ref)
    sizes = call[...].reshape(N, BLOCK).astype(F32)
    sizes16 = sizes.astype(BF16)
    n_col = jnp.sum(sizes, axis=1, keepdims=True)
    before64 = (iota((N, N), 1) < iota((N, N), 0)).astype(BF16)
    off_col = jnp.sum(jnp.dot(before64, sizes16, preferred_element_type=F32), axis=1, keepdims=True)
    upto = (iota((BLOCK, BLOCK), 0) <= iota((BLOCK, BLOCK), 1)).astype(BF16)
    block_end = off_col + jnp.dot(sizes16, upto, preferred_element_type=F32)
    drops = jnp.where(lane < NB, float(BLOCK + 1) - sizes, 1.0)
    logs = jnp.log(drops).astype(BF16).astype(F32)
    j_row = (iota((1, K_DEV), 1) * N + me).astype(F32)
    bias_out = jnp.zeros((N, K_DEV), F32)
    for b in range(NB):
        hit = (block_end[:, b : b + 1] - 1.0) == j_row
        bias_out = jnp.where(hit, logs[:, b : b + 1], bias_out)
    pb_ref[...] = jnp.sum(bias_out, axis=0).astype(BF16)
    last = ends.astype(I32) - 1
    pick = (iota((N, N), 1) == (last >> 4)).astype(F32)
    picked = jnp.dot(pick, block_end, preferred_element_type=F32, precision=lax.Precision.HIGHEST)
    req_end = jnp.sum(jnp.where(lane == (last & 15), picked, 0.0), axis=1, keepdims=True)
    past = ((req_end <= j_row) & ((iota((N, K_DEV), 0) & 7) < 6)).astype(F32)
    owner = jnp.sum(past, axis=0, keepdims=True)
    every = jnp.sum(n_col, axis=0, keepdims=True)
    pr_ref[...] = jnp.where(j_row < every, owner, -1.0).astype(I32)[0]

    off_i = off_col.astype(I32)
    c_col = (me - off_i) & (N - 1)
    k0_col = ((off_i + c_col) >> 6).astype(F32)
    lim_col = n_col - c_col.astype(F32)
    col = iota((N, MAIN), 1)
    is_src = iota((N, MAIN), 0) == (col >> 4)
    k0 = jnp.sum(jnp.where(is_src, k0_col, 0.0), axis=0, keepdims=True)
    lim = jnp.sum(jnp.where(is_src, lim_col, 0.0), axis=0, keepdims=True)
    q = (col[0:1, :] & (SLAB - 1)).astype(F32)
    tgt[...] = jnp.where(q * N < lim, k0 + q, -1.0).astype(I32)
    is_src = srow == lane
    k0 = jnp.sum(jnp.where(is_src, k0_col, 0.0), axis=0, keepdims=True)
    lim = jnp.sum(jnp.where(is_src, lim_col, 0.0), axis=0, keepdims=True)
    xtgt[...] = jnp.where(lim > float(MAIN), k0 + float(SLAB), -1.0).astype(I32)


def place_kernel(recv, xrecv, tgt, xtgt, pk_ref, pv_ref, x2):
    x2[...] = jnp.zeros(x2.shape, F32)

    def fill_extra(i, _):
        pair = xrecv[i].astype(F32)
        x2[pl.ds(i, 1), 0:HD] = pair[0:1, :]
        x2[pl.ds(i, 1), HD : 2 * HD] = pair[1:2, :]
        return 0

    lax.fori_loop(0, N, fill_extra, 0, unroll=8)

    def place(j, _):
        start = pl.multiple_of(j * TILE, 16)
        sel = jnp.where(iota((TILE, MAIN), 0) + start == tgt[...], 1.0, 0.0).astype(BF16)
        xsel = jnp.where(iota((TILE, BLOCK), 0) + start == xtgt[...], 1.0, 0.0).astype(BF16)
        rows = recv[...].reshape(MAIN, 2 * HD)
        got = jnp.dot(sel, rows, preferred_element_type=F32)
        got = got + jnp.dot(xsel, x2[...].astype(BF16), preferred_element_type=F32)
        pk_ref[pl.ds(start, TILE), :] = got[:, 0:HD].astype(BF16)
        pv_ref[pl.ds(start, TILE), :] = got[:, HD : 2 * HD].astype(BF16)
        return 0

    lax.fori_loop(0, TILES, place, 0)


def step_of(i):
    half = (i + 1) // 2
    return N // 2 + half * (1 - 2 * (i % 2))


def swap_kernel(
    counts, rsend, twice, xtwice, own_ref, ow_ref, req_ref,
    recv, xrecv, lo_ref, pb_ref, pr_ref, tgt, xtgt,
    call, send, xsend, prow, zsend, pcol, gsend, grecv, tsend, trecv,
    s_c, r_c, s_p, r_p, s_q, r_q, s_m, r_m, s_x, r_x, s_g, r_g, s_h, r_h, s_t, r_t,
):
    me = lax.axis_index("seq")
    mt = lax.axis_index("tp")
    z, x = lax.div(me, NX), lax.rem(me, NX)

    def seq_copy(src, dst, s_sem, r_sem, p):
        return pltpu.make_async_remote_copy(
            src, dst, s_sem, r_sem, device_id={"seq": p}, device_id_type=MESH
        )

    def tp_copy(src, dst, p):
        return pltpu.make_async_remote_copy(
            src, dst, s_t, r_t, device_id={"tp": p}, device_id_type=MESH
        )

    def partner(i):
        return lax.rem(me + step_of(i), N)

    def z_part(i):
        return lax.rem(z + 1 + i, NZ)

    def x_part(i):
        return lax.rem(x + 1 + i, NX)

    near = lax.rem(me + 1, N)
    barrier = pltpu.get_barrier_semaphore()

    def greet(i, _):
        pl.semaphore_signal(barrier, inc=1, device_id={"seq": partner(i)}, device_id_type=MESH)
        return 0

    lax.fori_loop(0, N - 1, greet, 0)

    def greet_tp(i, _):
        p = lax.rem(mt + 1 + i, TP)
        pl.semaphore_signal(barrier, inc=1, device_id={"tp": p}, device_id_type=MESH)
        return 0

    lax.fori_loop(0, TP - 1, greet_tp, 0)
    call[me] = counts[...]
    prow[x] = rsend[x]
    pl.semaphore_wait(barrier, N - 1 + TP - 1)

    def send_counts(i, _):
        seq_copy(counts, call.at[me], s_c, r_c, partner(i)).start()
        return 0

    lax.fori_loop(0, N - 1, send_counts, 0)

    def send_part(i, _):
        p = x_part(i)
        seq_copy(rsend.at[p], prow.at[x], s_p, r_p, z * NX + p).start()
        return 0

    lax.fori_loop(0, NX - 1, send_part, 0)

    all_c = call.at[pl.ds(0, N - 1)]
    seq_copy(all_c, all_c, s_c, r_c, near).wait_recv()
    earlier = lax.broadcasted_iota(I32, (N, 1, BLOCK), 0) < me
    offset = jnp.sum(jnp.sum(jnp.where(earlier, call[...], 0), axis=0))
    turn = (0 - offset) & (N - 1)
    send[...] = twice[pl.ds(turn, N)]
    xsend[...] = xtwice[pl.ds(turn, N)]

    def send_slab(i, _):
        p = partner(i)
        seq_copy(send.at[p], recv.at[me], s_m, r_m, p).start()
        seq_copy(xsend.at[p], xrecv.at[me], s_x, r_x, p).start()
        return 0

    lax.fori_loop(CUTS[0], CUTS[1], send_slab, 0)
    recv[me] = send[me]
    xrecv[me] = xsend[me]

    all_p = prow.at[pl.ds(0, NX - 1)]
    seq_copy(all_p, all_p, s_p, r_p, near).wait_recv()
    peaks = prow[:, :, :, HD : HD + 128]
    peak = jnp.max(peaks, axis=0)
    w = jnp.exp(peaks - peak[None])
    for c in (0, 1, 3):
        lanes = slice(128 * c, 128 * (c + 1))
        zsend[:, :, lanes] = jnp.sum(w * prow[:, :, :, lanes], axis=0)
    zsend[:, :, HD : HD + 128] = peak
    pcol[z] = zsend[z]

    def send_merged(i, _):
        p = z_part(i)
        seq_copy(zsend.at[p], pcol.at[z], s_q, r_q, p * NX + x).start()
        return 0

    lax.fori_loop(0, NZ - 1, send_merged, 0)
    lax.fori_loop(CUTS[1], CUTS[2], send_slab, 0)

    all_q = pcol.at[pl.ds(0, NZ - 1)]
    seq_copy(all_q, all_q, s_q, r_q, near).wait_recv()
    own = own_ref[:, HD : HD + 128]
    peaks = pcol[:, :, HD : HD + 128]
    peak = jnp.maximum(jnp.max(peaks, axis=0), own)
    w = jnp.exp(peaks - peak[None])
    own_p = jnp.exp(own - peak)
    tot = jnp.sum(w * pcol[:, :, HD + 128 : HD + 256], axis=0) + own_p
    for c in range(2):
        lanes = slice(128 * c, 128 * (c + 1))
        wsum = jnp.sum(w * pcol[:, :, lanes], axis=0) + own_p * own_ref[:, lanes]
        gsend[:, lanes] = (wsum / tot).astype(BF16).astype(F32)
    grecv[x, z] = gsend[...]

    def send_row(i, _):
        seq_copy(gsend, grecv.at[x, z], s_g, r_g, z_part(i) * NX + x).start()
        return 0

    lax.fori_loop(0, NZ - 1, send_row, 0)
    lax.fori_loop(CUTS[2], CUTS[3], send_slab, 0)

    all_g = grecv.at[0, pl.ds(0, NZ - 1)]
    seq_copy(all_g, all_g, s_g, r_g, near).wait_recv()

    def send_rows(i, _):
        seq_copy(grecv.at[x], grecv.at[x], s_h, r_h, z * NX + x_part(i)).start()
        return 0

    lax.fori_loop(0, NX - 1, send_rows, 0)
    lax.fori_loop(CUTS[3], CUTS[4], send_slab, 0)

    all_h = grecv.at[pl.ds(0, NX - 1)]
    seq_copy(all_h, all_h, s_h, r_h, near).wait_recv()
    rows = grecv[...].reshape(N, HD).astype(BF16)
    wide = lax.dot_general(rows, ow_ref[...], (((1,), (1,)), ((), ())), preferred_element_type=F32)
    wide = jnp.concatenate([wide, jnp.zeros((N, 96), F32)], axis=1)
    tsend[...] = wide.reshape(TP, 8, 128)
    trecv[mt] = tsend[mt]

    def send_tp(i, _):
        p = lax.rem(mt + 1 + i, TP)
        tp_copy(tsend.at[p], trecv.at[mt], p).start()
        return 0

    lax.fori_loop(0, TP - 1, send_tp, 0)
    lax.fori_loop(CUTS[4], CUTS[5], send_slab, 0)
    slot_tables(call, req_ref, me, pb_ref, pr_ref, tgt, xtgt)

    all_t = trecv.at[pl.ds(0, TP - 1)]
    tp_copy(all_t, all_t, lax.rem(mt + 1, TP)).wait_recv()
    lo_ref[...] = jnp.sum(trecv[...], axis=0)[0:6, 0:32].astype(BF16)

    all_m = recv.at[pl.ds(0, N - 1)]
    all_x = xrecv.at[pl.ds(0, N - 1)]
    for part, s_sem, r_sem in ((all_m, s_m, r_m), (all_x, s_x, r_x)):
        seq_copy(part, part, s_sem, r_sem, near).wait_recv()
    for part, s_sem, r_sem in (
        (all_c, s_c, r_c), (all_p, s_p, r_p), (all_q, s_q, r_q), (all_g, s_g, r_g),
        (all_h, s_h, r_h), (all_m, s_m, r_m), (all_x, s_x, r_x),
    ):
        seq_copy(part, part, s_sem, r_sem, near).wait_send()
    tp_copy(all_t, all_t, lax.rem(mt + 1, TP)).wait_send()


def exchange(counts, rsend, twice, xtwice, own, ow, req):
    vmem = pl.BlockSpec(memory_space=pltpu.VMEM)
    outs = [
        ((N, SLAB, 2 * HD), BF16), ((N, 2, HD), BF16), ((6, 32), BF16),
        ((K_DEV,), BF16), ((K_DEV,), I32), ((1, MAIN), I32), ((1, BLOCK), I32),
    ]
    scratch = [
        ((N, 1, BLOCK), I32),
        ((N, SLAB, 2 * HD), BF16),
        ((N, 2, HD), BF16),
        ((NX, NZ, 1, 2 * HD), F32),
        ((NZ, 1, 2 * HD), F32),
        ((NZ, 1, 2 * HD), F32),
        ((1, HD), F32),
        ((NX, NZ, 1, HD), F32),
        ((TP, 8, 128), F32),
        ((TP, 8, 128), F32),
    ]
    return pl.pallas_call(
        swap_kernel,
        name="swap",
        out_shape=tuple(jax.ShapeDtypeStruct(s, d) for s, d in outs),
        in_specs=[vmem] * 7,
        out_specs=(vmem,) * len(outs),
        scratch_shapes=[pltpu.VMEM(s, d) for s, d in scratch] + [pltpu.SemaphoreType.DMA] * 16,
        compiler_params=pltpu.CompilerParams(
            collective_id=0, has_side_effects=True, vmem_limit_bytes=40 << 20
        ),
    )(counts, rsend, twice, xtwice, own, ow, req)


def local(body, name, outs, scratch, *args, fetch=False):
    vmem = pl.BlockSpec(memory_space=pltpu.VMEM)
    whole = {"in_specs": [vmem] * len(args)}
    if fetch:
        args = [pltpu.with_memory_space_constraint(a, pltpu.HBM) for a in args]
        whole = {
            "grid": (1,),
            "in_specs": [pl.BlockSpec(a.shape, lambda i: (0, 0)) for a in args],
        }
    return pl.pallas_call(
        body,
        name=name,
        out_shape=tuple(jax.ShapeDtypeStruct(s, d) for s, d in outs),
        out_specs=(vmem,) * len(outs),
        scratch_shapes=[pltpu.VMEM(s, d) for s, d in scratch],
        compiler_params=pltpu.CompilerParams(vmem_limit_bytes=40 << 20),
        **whole,
    )(*args)


def on_device(ck, cv, keep, w, req, q, nk, nv, ow):
    keep2 = keep.reshape(NB, BLOCK)
    w2 = w.reshape(NB, BLOCK)
    req2 = req.reshape(1, REQS)
    twice, xtwice, counts, rsend, own = local(
        pack_kernel, "pack",
        [
            ((2 * N, SLAB, 2 * HD), BF16), ((2 * N, 2, HD), BF16), ((1, BLOCK), I32),
            ((NX, NZ, 1, 2 * HD), F32), ((1, HD + 128), F32),
        ],
        [((K_DEV, 2 * HD), BF16), ((N, 2 * HD), F32), ((K_DEV - MAIN, 2 * HD), F32)],
        ck, cv, keep2, w2, req2, q, nk, nv,
        fetch=True,
    )
    recv, xrecv, lo, pb, pr, tgt, xtgt = exchange(counts, rsend, twice, xtwice, own, ow.T, req2)
    pk, pv = local(
        place_kernel, "place",
        [((K_DEV, HD), BF16), ((K_DEV, HD), BF16)], [((BLOCK, 2 * HD), F32)],
        recv, xrecv, tgt, xtgt,
    )
    return pk, pv, pb, pr, lo


def solution(mesh):
    in_specs = (
        P("seq", "tp"), P("seq", "tp"), P("seq"), P("seq"), P(),
        P(None, "tp"), P(None, "tp"), P(None, "tp"), P("tp", "seq"),
    )
    out_specs = (P("seq", "tp"), P("seq", "tp"), P("seq"), P("seq"), P("tp", "seq"))
    return jax.shard_map(on_device, mesh=mesh, in_specs=in_specs, out_specs=out_specs, check_vma=False)
```
